256 devices in a mesh: dp: 64 (over x, y_hi, z), seq: 4 (over y_lo, core).
Axes of the slice: x: 4, y: 4 (y_hi: 2, y_lo: 2; y = y_hi * 2 + y_lo), z: 8, core: 2. Of those that a mesh axis runs over, the one named last changes fastest.
Arguments:
- queries: bfloat16 [64, 512, 768], P('dp', 'seq'), may hold values from -720 to 720
- key_rows: bfloat16 [64, 512, 768], P('dp', 'seq'), may hold values from -7 to 7
- value_rows: bfloat16 [64, 512, 768], P('dp', 'seq'), may hold values from -6 to 6
- conv_weight: bfloat16 [768, 3, 768], replicated, may hold values from -0.125 to 0.125
- output_gradient: bfloat16 [64, 512, 768], P('dp', 'seq'), may hold values from -16 to 16
Outputs:
- conv_out: bfloat16 [64, 512, 768], P('dp', 'seq')
- grad_queries: bfloat16 [64, 512, 768], P('dp', 'seq')
- grad_keys: bfloat16 [64, 512, 768], P('dp', 'seq')
- grad_values: bfloat16 [64, 512, 768], P('dp', 'seq')
- grad_weight: float32 [768, 3, 768], P('dp', None, 'seq')
The draws below stay inside these ranges and needn't reach their ends.
All inputs are finite; a program needn't handle non-finite values.
Results may differ from the reference program's by a relative error of at most 0.014.
Values may be sent and summed in bfloat16 or wider, within the bound.
No kernel may reach another device: no remote copies, remote signals or barrier semaphores. Data moves between devices by JAX's collectives and lax.ppermute only.
A program may use at most 64 MiB of HBM per device.

```python
import math
import jax
import jax.numpy as jnp
from jax import lax

D = 768
HEADS = 4
HEAD_DIM = 192
CH = 768
TAPS = 3
DILATION_STEP = 32
SEQUENCE_LENGTH = 512
SEQS = 64


def drawn_draws(key):
    shape = (SEQS, SEQUENCE_LENGTH, D)
    query_base = jnp.clip(jax.random.normal(jax.random.fold_in(key, 11), shape, jnp.float32), -6.0, 6.0)
    key_base = jnp.clip(jax.random.normal(jax.random.fold_in(key, 12), shape, jnp.float32), -6.0, 6.0)
    return (query_base, key_base)


def draw_queries(key, part):
    return drawn_draws(key)[0].astype(jnp.bfloat16)


def draw_key_rows(key, part):
    return drawn_draws(key)[1].astype(jnp.bfloat16)


def with_spikes(drawn, rng, source, target, blocks, factor):
    owner, partner = [(jnp.arange(drawn.shape[axis_at]) // (drawn.shape[axis_at] // blocks)).reshape([-1 if axis == axis_at else 1 for axis in range(drawn.ndim)]) for axis_at in (source, target)]
    chosen = jax.random.permutation(rng, blocks)[partner]
    strong = (owner == chosen) | (owner == (partner + blocks // 2) % blocks)
    return jnp.where(strong, factor * drawn, drawn)


def block_scale(stream_key, dims, cuts, least, high):
    level, own = 1.0, jax.random.fold_in(stream_key, 6)
    for dim, parts in cuts:
        draws = jnp.exp(jax.random.uniform(jax.random.fold_in(own, dim), (parts,), jnp.float32, least / len(cuts), high / len(cuts)))
        level = level * jnp.repeat(draws, dims[dim] // parts).reshape([-1 if axis == dim else 1 for axis in range(len(dims))])
    return level


def centred(rng, shape, scale, bound, cuts=(), held_as=jnp.bfloat16):
    entries = scale * jax.random.normal(rng, shape, jnp.float32)
    if cuts:
        entries = entries * block_scale(rng, shape, cuts, -0.22, 0.18)
    return jnp.clip(entries, -bound, bound).astype(held_as)


def heavy_noise(stream_key, extent, deviation, limit, cuts, heavy, dtype=jnp.bfloat16):
    values = deviation * jax.random.normal(stream_key, extent, jnp.float32)
    if cuts:
        values = values * block_scale(stream_key, extent, cuts, -0.22, 0.18)
    return jnp.clip(with_spikes(values, jax.random.fold_in(stream_key, 3), *heavy), -limit, limit).astype(dtype)


def setup_inputs(seed: int = 0) -> dict:
    key_list = jax.random.split(jax.random.key(seed), 6)
    queries = draw_queries(jax.random.fold_in(key_list[5], 71), 0)
    key_rows = draw_key_rows(jax.random.fold_in(key_list[5], 71), 0)
    value_rows = centred(key_list[2], (SEQS, SEQUENCE_LENGTH, D), 1.0, 6.0, ((0, 64), (1, 4)))
    conv_weight = centred(key_list[3], (D, TAPS, CH), (TAPS * D) ** -0.5, 0.125)
    output_gradient = heavy_noise(key_list[4], (SEQS, SEQUENCE_LENGTH, CH), 1.0, 16.0, ((0, 64), (1, 4)), (0, 2, 64, 4.0))
    return {"queries": queries, "key_rows": key_rows, "value_rows": value_rows, "conv_weight": conv_weight, "output_gradient": output_gradient}


tanh_scale = 0.7978845608028654
cubic_term = 0.044715
norm_epsilon = 1e-06

def gelu_pair(value):
    inner = tanh_scale * (value + cubic_term * value * value * value)
    tangent = jnp.tanh(inner)
    result = 0.5 * value * (1.0 + tangent)
    slope = 0.5 * (1.0 + tangent) + 0.5 * value * (1.0 - tangent * tangent) * tanh_scale * (1.0 + 3.0 * cubic_term * value * value)
    return (result, slope)

def reference(queries, key_rows, value_rows, conv_weight, output_gradient):
    inverse = 1.0 / math.sqrt(HEAD_DIM)
    grad_scale = 1.0 / math.sqrt(SEQS * SEQUENCE_LENGTH)

    def per_sequence(running_sum, inputs):
        query, keys, values, incoming_gradient = inputs
        query_heads = query.astype(jnp.float32).reshape(SEQUENCE_LENGTH, HEADS, HEAD_DIM)
        key_heads = keys.astype(jnp.float32).reshape(SEQUENCE_LENGTH, HEADS, HEAD_DIM)
        value_heads = values.astype(jnp.float32).reshape(SEQUENCE_LENGTH, HEADS, HEAD_DIM)
        scores = jnp.einsum('qhd,khd->hqk', query_heads, key_heads) * inverse
        soft_exact = jax.nn.softmax(scores, axis=-1)
        soft_rounded = lax.optimization_barrier(soft_exact.astype(jnp.bfloat16)).astype(jnp.float32)
        attended = jnp.einsum('hqk,khd->qhd', soft_rounded, value_heads).reshape(SEQUENCE_LENGTH, D).astype(jnp.bfloat16)
        att_full = attended.astype(jnp.float32)
        mean_square = lax.optimization_barrier(jnp.mean(att_full * att_full, axis=-1, keepdims=True))
        norm_factor = lax.rsqrt(mean_square + norm_epsilon)
        normed = att_full * norm_factor
        gelu_value, gelu_slope = gelu_pair(normed)
        activation_output = gelu_value.astype(jnp.bfloat16)
        padded_input = jnp.pad(activation_output, ((DILATION_STEP, DILATION_STEP), (0, 0)))
        padded_gradient = jnp.pad(incoming_gradient, ((DILATION_STEP, DILATION_STEP), (0, 0)))
        conv_sum = jnp.zeros((SEQUENCE_LENGTH, CH), jnp.float32)
        grad_acted = jnp.zeros((SEQUENCE_LENGTH, D), jnp.float32)
        tap_terms = []
        for kernel_tap_index in range(TAPS):
            shifted_input = padded_input[kernel_tap_index * DILATION_STEP:kernel_tap_index * DILATION_STEP + SEQUENCE_LENGTH]
            conv_sum = conv_sum + jnp.dot(shifted_input, conv_weight[:, kernel_tap_index, :], preferred_element_type=jnp.float32)
            reverse_rows = padded_gradient[(2 - kernel_tap_index) * DILATION_STEP:(2 - kernel_tap_index) * DILATION_STEP + SEQUENCE_LENGTH]
            grad_acted = grad_acted + jnp.dot(reverse_rows, conv_weight[:, kernel_tap_index, :].T, preferred_element_type=jnp.float32)
            tap_terms.append(jnp.dot(shifted_input.T, incoming_gradient, preferred_element_type=jnp.float32))
        local_term = jnp.stack(tap_terms, axis=1)
        conv_out = conv_sum.astype(jnp.bfloat16)
        grad_normed = grad_acted * gelu_slope
        mean_inner = lax.optimization_barrier(jnp.mean(grad_normed * normed, axis=-1, keepdims=True))
        grad_attended = (norm_factor * (grad_normed - normed * mean_inner)).astype(jnp.bfloat16)
        grad_heads = grad_attended.astype(jnp.float32).reshape(SEQUENCE_LENGTH, HEADS, HEAD_DIM)
        grad_values = jnp.einsum('hqk,qhd->khd', soft_rounded, grad_heads).reshape(SEQUENCE_LENGTH, D)
        grad_soft = jnp.einsum('qhd,khd->hqk', grad_heads, value_heads)
        row_inner = lax.optimization_barrier(jnp.sum(grad_soft * soft_exact, axis=-1, keepdims=True))
        grad_scores = lax.optimization_barrier((soft_exact * (grad_soft - row_inner) * inverse).astype(jnp.bfloat16)).astype(jnp.float32)
        grad_queries = jnp.einsum('hqk,khd->qhd', grad_scores, key_heads).reshape(SEQUENCE_LENGTH, D)
        grad_keys = jnp.einsum('hqk,qhd->khd', grad_scores, query_heads).reshape(SEQUENCE_LENGTH, D)
        results = (conv_out, grad_queries.astype(jnp.bfloat16), grad_keys.astype(jnp.bfloat16), grad_values.astype(jnp.bfloat16))
        return (running_sum + local_term, results)
    initial = jnp.zeros((D, TAPS, CH), jnp.float32)
    total_term, stacked = lax.scan(per_sequence, initial, (queries, key_rows, value_rows, output_gradient))
    return (stacked[0], stacked[1], stacked[2], stacked[3], total_term * grad_scale)
```

```python
import math

import jax
import jax.numpy as jnp
from jax import lax
from jax.experimental import pallas as pl
from jax.experimental.pallas import tpu as pltpu
from jax.sharding import Mesh, PartitionSpec as P

HEADS = 4
HEAD_DIM = 192
TAPS = 3
STEP = 32
ROWS = 128
SPLITS = {64: (4, 2, 8), 4: (1, 2, 2)}

tanh_scale = 0.7978845608028654
cubic_term = 0.044715
norm_epsilon = 1e-06

F32 = jnp.float32
BF16 = jnp.bfloat16
WINDOW = (0, 128, 384, 512)
FIRST = (0, 64, 0, 64)
NT = (((1,), (1,)), ((), ()))
TN = (((0,), (0,)), ((), ()))


def dot(a, b, dims=(((1,), (0,)), ((), ()))):
    return lax.dot_general(a, b, dims, preferred_element_type=F32)


def masked_window(value, head):
    lane = lax.broadcasted_iota(jnp.int32, value.shape, 1)
    first = FIRST[head]
    keep = (lane >= first) & (lane < first + HEAD_DIM)
    return jnp.where(keep, value, jnp.zeros_like(value))


def window(ref, head):
    return ref[:, WINDOW[head] : WINDOW[head] + 256]


def place(parts):
    a, b, c, d = parts
    return jnp.concatenate(
        [
            a[:, :128],
            a[:, 128:] + b[:, :128],
            b[:, 128:],
            c[:, :128],
            c[:, 128:] + d[:, :128],
            d[:, 128:],
        ],
        axis=1,
    )


def gelu_value(value):
    inner = tanh_scale * (value + cubic_term * value * value * value)
    return 0.5 * value * (1.0 + jnp.tanh(inner))


def gelu_slope(value):
    square = value * value
    tangent = jnp.tanh(tanh_scale * (value + cubic_term * square * value))
    return 0.5 * (1.0 + tangent) + 0.5 * value * (1.0 - tangent * tangent) * tanh_scale * (
        1.0 + 3.0 * cubic_term * square
    )


def block_start(me, relative):
    return pl.multiple_of(jnp.bitwise_xor(me, relative) * ROWS, ROWS)


def forward_kernel(ids, *refs):
    q, k, v = refs[0:4], refs[4:8], refs[8:12]
    soft_ref, attended_ref, acted_ref = refs[12:15]
    q_all, km, vm, s_ref, p_ref, o_ref = refs[15:]
    me = ids[0]
    inverse = 1.0 / math.sqrt(HEAD_DIM)
    for r in range(4):
        at = slice(r * ROWS, (r + 1) * ROWS)
        q_all[at, :] = q[r][...]
        for h in range(HEADS):
            km[h, at, :] = masked_window(window(k[r], h), h)
            vm[h, at, :] = masked_window(window(v[r], h), h)
    for h in range(HEADS):
        s_ref[...] = dot(window(q_all, h), km[h], NT)
        for c in range(8):
            at = slice(c * 64, (c + 1) * 64)
            s = s_ref[at, :] * inverse
            e = jnp.exp(s - jnp.max(s, axis=1, keepdims=True))
            p = e / jnp.sum(e, axis=1, keepdims=True)
            soft_ref[h, at, :] = p
            p_ref[at, :] = p.astype(BF16)
        o_ref[h] = dot(p_ref[...], vm[h])
    acted_ref[0:STEP, :] = jnp.zeros((STEP, 768), BF16)
    acted_ref[STEP + 512 :, :] = jnp.zeros((STEP, 768), BF16)
    for r in range(4):
        at = slice(r * ROWS, (r + 1) * ROWS)
        attended = place([o_ref[h, at, :] for h in range(HEADS)]).astype(BF16)
        attended_ref[at, :] = attended
        full = attended.astype(F32)
        factor = lax.rsqrt(jnp.mean(full * full, axis=1, keepdims=True) + norm_epsilon)
        start = pl.multiple_of(block_start(me, r) + STEP, STEP)
        acted_ref[pl.ds(start, ROWS), :] = gelu_value(full * factor).astype(BF16)


def weight_kernel(ids, acted_ref, g0, g1, g2, g3, *refs):
    outs, (slab, shifted, total) = refs[:-3], refs[-3:]
    me, mx = ids[0], ids[1]
    parts = len(outs)
    slab[0:STEP, :] = jnp.zeros((STEP, HEAD_DIM), BF16)
    slab[STEP + 512 :, :] = jnp.zeros((STEP, HEAD_DIM), BF16)
    for r, g in enumerate((g0, g1, g2, g3)):
        mine = g[:, 0:192].astype(F32)
        for s in range(1, 4):
            mine = jnp.where(me == s, g[:, 192 * s : 192 * s + 192].astype(F32), mine)
        start = pl.multiple_of(block_start(me, r) + STEP, STEP)
        slab[pl.ds(start, ROWS), :] = mine.astype(BF16)
    for t in range(TAPS):
        first = (2 - t) * STEP
        shifted[:, 192 * t : 192 * t + 192] = slab[first : first + 512, :]
    result = dot(acted_ref[STEP : STEP + 512, :], shifted[...], TN)
    rows = 768 // parts
    half = rows // 2
    for j in range(parts):
        total[j] = result[j * rows : (j + 1) * rows]
    for n, out in enumerate(outs):
        piece = total[lax.rem(mx + n, parts)]
        out[...] = jnp.concatenate([piece[:half], piece[half:]], axis=1).astype(BF16)


def backward_kernel(ids, *refs):
    q, k, v, g = refs[0:4], refs[4:8], refs[8:12], refs[12:16]
    soft_ref, attended_ref, acted_ref, w_ref = refs[16:20]
    conv_ref, dq_ref, dk_ref, dv_ref = refs[20:24]
    km, vm, qm, g_pad, ga_ref, do_ref, dp_ref, ds_ref = refs[24:]
    me = ids[0]
    inverse = 1.0 / math.sqrt(HEAD_DIM)
    own = pl.multiple_of(me * ROWS, ROWS)
    conv = jnp.zeros((ROWS, 768), F32)
    for t in range(TAPS):
        rows = acted_ref[pl.ds(pl.multiple_of(own + t * STEP, STEP), ROWS), :]
        conv = conv + dot(rows, w_ref[t])
    conv_ref[...] = conv.astype(BF16)
    g_pad[0:STEP, :] = jnp.zeros((STEP, 768), BF16)
    g_pad[STEP + 512 :, :] = jnp.zeros((STEP, 768), BF16)
    for r in range(4):
        at = slice(r * ROWS, (r + 1) * ROWS)
        start = pl.multiple_of(block_start(me, r) + STEP, STEP)
        g_pad[pl.ds(start, ROWS), :] = g[r][...]
        for h in range(HEADS):
            km[h, at, :] = masked_window(window(k[r], h), h)
            vm[h, at, :] = masked_window(window(v[r], h), h)
            qm[h, at, :] = masked_window(window(q[r], h), h)
    ga_ref[...] = dot(g_pad[2 * STEP : 2 * STEP + 512, :], w_ref[0], NT)
    ga_ref[...] += dot(g_pad[STEP : STEP + 512, :], w_ref[1], NT)
    ga_ref[...] += dot(g_pad[0:512, :], w_ref[2], NT)
    for r in range(4):
        at = slice(r * ROWS, (r + 1) * ROWS)
        full = attended_ref[at, :].astype(F32)
        factor = lax.rsqrt(jnp.mean(full * full, axis=1, keepdims=True) + norm_epsilon)
        normed = full * factor
        grad = ga_ref[pl.ds(block_start(me, r), ROWS), :] * gelu_slope(normed)
        inner = jnp.mean(grad * normed, axis=1, keepdims=True)
        do_ref[at, :] = (factor * (grad - normed * inner)).astype(BF16)
    dq, dk, dv = [], [], []
    for h in range(HEADS):
        grad_out = window(do_ref, h)
        dp_ref[...] = dot(grad_out, vm[h], NT)
        for c in range(8):
            at = slice(c * 64, (c + 1) * 64)
            p = soft_ref[h, at, :]
            dp = dp_ref[at, :]
            inner = jnp.sum(dp * p, axis=1, keepdims=True)
            wide = 512 if c < 2 else ROWS
            ds_ref[at, 0:wide] = (p[:, :wide] * (dp[:, :wide] - inner) * inverse).astype(BF16)
        dq.append(dot(ds_ref[0:ROWS, :], km[h]))
        dk.append(dot(ds_ref[:, 0:ROWS], qm[h], TN))
        dv.append(dot(soft_ref[h, :, 0:ROWS].astype(BF16), masked_window(grad_out, h), TN))
    dq_ref[...] = place(dq).astype(BF16)
    dk_ref[...] = place(dk).astype(BF16)
    dv_ref[...] = place(dv).astype(BF16)


def sum_kernel(ids, *refs):
    parts, outs, total = refs[: ids_parts(refs)], refs[ids_parts(refs) : -1], refs[-1]
    mz = ids[2]
    value = parts[0][...].astype(F32)
    for part in parts[1:]:
        value = value + part[...].astype(F32)
    count = len(outs)
    rows = value.shape[0] // count
    for j in range(count):
        total[j, 0:rows, :] = value[j * rows : (j + 1) * rows]
    for n, out in enumerate(outs):
        out[...] = total[lax.rem(mz + n, count), 0:rows, :].astype(BF16)


def ids_parts(refs):
    shape = refs[0].shape
    count = 0
    while refs[count].shape == shape and count < len(refs) - 1:
        count += 1
    return count


def half_kernel(ids, *refs):
    parts, (keep_ref, send_ref) = refs[:-2], refs[-2:]
    my = ids[3]
    value = parts[0][...].astype(F32)
    for part in parts[1:]:
        value = value + part[...].astype(F32)
    low, high = value[:, :576], value[:, 576:]
    keep_ref[...] = jnp.where(my == 0, low, high)
    send_ref[...] = jnp.where(my == 0, high, low).astype(BF16)


def last_kernel(scale, keep_ref, got_ref, out_ref):
    value = (keep_ref[...] + got_ref[...].astype(F32)) * scale
    for t in range(TAPS):
        out_ref[:, t, :] = value[:, 192 * t : 192 * t + 192]


def call(kernel, outs, scratch, args, flops, limit=24):
    size = sum(math.prod(a.shape) * a.dtype.itemsize for a in (*args, *outs))
    return pl.pallas_call(
        kernel,
        out_shape=outs,
        in_specs=[
            pl.BlockSpec(memory_space=pltpu.SMEM if a.dtype == jnp.int32 else pltpu.VMEM)
            for a in args
        ],
        out_specs=[pl.BlockSpec(memory_space=pltpu.VMEM) for _ in outs],
        scratch_shapes=scratch,
        compiler_params=pltpu.CompilerParams(vmem_limit_bytes=limit << 20),
        cost_estimate=pl.CostEstimate(
            flops=flops, bytes_accessed=size, transcendentals=0
        ),
    )(*args)


def shaped(shape, dtype=BF16):
    return jax.ShapeDtypeStruct(shape, dtype)


def shift(value, axis, by):
    count = lax.axis_size(axis)
    return lax.ppermute(value, axis, [(i, (i + by) % count) for i in range(count)])


def blocks(value):
    across = shift(value, "yl", 1)
    return value, shift(value, "core", 1), across, shift(across, "core", 1)


def body(queries, key_rows, value_rows, conv_weight, output_gradient):
    x_size, z_size = lax.axis_size("x"), lax.axis_size("z")
    sizes = [lax.axis_size(a) for a in ("x", "yh", "z", "yl", "core")]
    grad_scale = 1.0 / math.sqrt(math.prod(sizes) * ROWS)
    me = lax.axis_index("yl") * 2 + lax.axis_index("core")
    ids = jnp.stack(
        [me, lax.axis_index("x"), lax.axis_index("z"), lax.axis_index("yh")]
    ).astype(jnp.int32)
    weight = jnp.transpose(conv_weight, (1, 0, 2))
    k = blocks(key_rows[0])
    q = blocks(queries[0])
    v = blocks(value_rows[0])
    g = blocks(output_gradient[0])
    soft, attended, acted = call(
        forward_kernel,
        [shaped((HEADS, 512, 512), F32), shaped((512, 768)), shaped((576, 768))],
        [
            pltpu.VMEM((512, 768), BF16),
            pltpu.VMEM((HEADS, 512, 256), BF16),
            pltpu.VMEM((HEADS, 512, 256), BF16),
            pltpu.VMEM((512, 512), F32),
            pltpu.VMEM((512, 512), BF16),
            pltpu.VMEM((HEADS, 512, 256), F32),
        ],
        [ids, *q, *k, *v],
        2_000_000_000,
    )
    rows = 768 // x_size
    pieces = call(
        weight_kernel,
        [shaped((rows // 2, 1152)) for _ in range(x_size)],
        [
            pltpu.VMEM((576, HEAD_DIM), BF16),
            pltpu.VMEM((512, 576), BF16),
            pltpu.VMEM((x_size, rows, 576), F32),
        ],
        [ids, acted, *g],
        500_000_000,
    )
    got = [pieces[0]] + [shift(pieces[n], "x", n) for n in range(1, x_size)]
    conv_out, grad_queries, grad_keys, grad_values = call(
        backward_kernel,
        [shaped((ROWS, 768)) for _ in range(4)],
        [
            pltpu.VMEM((HEADS, 512, 256), BF16),
            pltpu.VMEM((HEADS, 512, 256), BF16),
            pltpu.VMEM((HEADS, 512, 256), BF16),
            pltpu.VMEM((576, 768), BF16),
            pltpu.VMEM((512, 768), F32),
            pltpu.VMEM((512, 768), BF16),
            pltpu.VMEM((512, 512), F32),
            pltpu.VMEM((512, 512), BF16),
        ],
        [ids, *q, *k, *v, *g, soft, attended, acted, weight],
        4_000_000_000,
        36,
    )
    few = rows // 2 // z_size
    pieces = call(
        sum_kernel,
        [shaped((few, 1152)) for _ in range(z_size)],
        [pltpu.VMEM((z_size, -(-few // 8) * 8, 1152), F32)],
        [ids, *got],
        1_000_000,
    )
    got = [pieces[0]] + [shift(pieces[n], "z", n) for n in range(1, z_size)]
    keep, send = call(
        half_kernel, [shaped((few, 576), F32), shaped((few, 576))], [], [ids, *got], 1_000_000
    )
    other = shift(send, "yh", 1)
    (grad_weight,) = call(
        lambda *refs: last_kernel(grad_scale, *refs),
        [shaped((few, TAPS, HEAD_DIM), F32)],
        [],
        [keep, other],
        1_000_000,
    )
    return conv_out[None], grad_queries[None], grad_keys[None], grad_values[None], grad_weight


def solution(mesh):
    x, yh, z = SPLITS[mesh.shape["dp"]]
    fine = Mesh(mesh.devices.reshape(x, yh, z, 2, 2), ("x", "yh", "z", "yl", "core"))
    dp, seq = ("x", "yh", "z"), ("yl", "core")
    return jax.shard_map(
        body,
        mesh=fine,
        in_specs=(P(dp, seq, None), P(dp, seq, None), P(dp, seq, None), P(), P(dp, seq, None)),
        out_specs=(
            P(dp, seq, None),
            P(dp, seq, None),
            P(dp, seq, None),
            P(dp, seq, None),
            P(dp, None, seq),
        ),
        check_vma=False,
    )
```

```python
import math

import jax
import jax.numpy as jnp
from jax import lax
from jax.experimental import pallas as pl
from jax.experimental.pallas import tpu as pltpu
from jax.sharding import Mesh, PartitionSpec as P


HEADS = 4
HEAD_DIM = 192
TAPS = 3
STEP = 32
ROWS = 128
SPLITS = {64: (4, 2, 8), 4: (1, 2, 2)}

tanh_scale = 0.7978845608028654
cubic_term = 0.044715
norm_epsilon = 1e-06

F32 = jnp.float32
BF16 = jnp.bfloat16
WINDOW = (0, 128, 384, 512)
FIRST = (0, 64, 0, 64)
NT = (((1,), (1,)), ((), ()))
TN = (((0,), (0,)), ((), ()))


def dot(a, b, dims=(((1,), (0,)), ((), ()))):
    return lax.dot_general(a, b, dims, preferred_element_type=F32)


def masked_window(value, head):
    lane = lax.broadcasted_iota(jnp.int32, value.shape, 1)
    first = FIRST[head]
    keep = (lane >= first) & (lane < first + HEAD_DIM)
    return jnp.where(keep, value, jnp.zeros_like(value))


def window(ref, head):
    return ref[:, WINDOW[head] : WINDOW[head] + 256]


def place(parts):
    a, b, c, d = parts
    return jnp.concatenate(
        [
            a[:, :128],
            a[:, 128:] + b[:, :128],
            b[:, 128:],
            c[:, :128],
            c[:, 128:] + d[:, :128],
            d[:, 128:],
        ],
        axis=1,
    )


def gelu_value(value):
    inner = tanh_scale * (value + cubic_term * value * value * value)
    return 0.5 * value * (1.0 + jnp.tanh(inner))


def gelu_slope(value):
    square = value * value
    tangent = jnp.tanh(tanh_scale * (value + cubic_term * square * value))
    return 0.5 * (1.0 + tangent) + 0.5 * value * (1.0 - tangent * tangent) * tanh_scale * (
        1.0 + 3.0 * cubic_term * square
    )


def block_start(me, relative):
    return pl.multiple_of(jnp.bitwise_xor(me, relative) * ROWS, ROWS)


def forward_kernel(ids, *refs):
    q, k, v = refs[0:4], refs[4:8], refs[8:12]
    soft_ref, attended_ref, acted_ref = refs[12:15]
    q_all, km, vm, s_ref, p_ref, o_ref, own, sems = refs[15:]
    me = ids[0]
    inverse = 1.0 / math.sqrt(HEAD_DIM)
    copies = [
        pltpu.make_async_copy(source, own.at[n], sems.at[n])
        for n, source in enumerate((q[0], k[0], v[0]))
    ]
    for copy in copies:
        copy.start()
    for r in (1, 2, 3, 0):
        at = slice(r * ROWS, (r + 1) * ROWS)
        if r == 0:
            for copy in copies:
                copy.wait()
            q_block, k_block, v_block = own.at[0], own.at[1], own.at[2]
        else:
            q_block, k_block, v_block = q[r], k[r], v[r]
        q_all[at, :] = q_block[...]
        for h in range(HEADS):
            km[h, at, :] = masked_window(window(k_block, h), h)
            vm[h, at, :] = masked_window(window(v_block, h), h)
    for h in range(HEADS):
        s_ref[...] = dot(window(q_all, h), km[h], NT)
        for c in range(8):
            at = slice(c * 64, (c + 1) * 64)
            s = s_ref[at, :] * inverse
            e = jnp.exp(s - jnp.max(s, axis=1, keepdims=True))
            p = e / jnp.sum(e, axis=1, keepdims=True)
            soft_ref[h, at, :] = p
            p_ref[at, :] = p.astype(BF16)
        o_ref[h] = dot(p_ref[...], vm[h])
    acted_ref[0:STEP, :] = jnp.zeros((STEP, 768), BF16)
    acted_ref[STEP + 512 :, :] = jnp.zeros((STEP, 768), BF16)
    for r in range(4):
        at = slice(r * ROWS, (r + 1) * ROWS)
        attended = place([o_ref[h, at, :] for h in range(HEADS)]).astype(BF16)
        attended_ref[at, :] = attended
        full = attended.astype(F32)
        factor = lax.rsqrt(jnp.mean(full * full, axis=1, keepdims=True) + norm_epsilon)
        start = pl.multiple_of(block_start(me, r) + STEP, STEP)
        acted_ref[pl.ds(start, ROWS), :] = gelu_value(full * factor).astype(BF16)


def weight_kernel(ids, acted_ref, g_own, g_core, g_across, g_diag, *refs):
    outs, (slab, shifted, total) = refs[:-3], refs[-3:]
    me, mx = ids[0], ids[1]
    parts = len(outs)
    slab[0:STEP, :] = jnp.zeros((STEP, HEAD_DIM), BF16)
    slab[STEP + 512 :, :] = jnp.zeros((STEP, HEAD_DIM), BF16)
    for r, g in enumerate((g_own, g_core, g_across, g_diag)):
        mine = g[:, 0:192].astype(F32)
        count = g.shape[1] // HEAD_DIM
        for s in range(1, count):
            here = lax.rem(me, count) == s
            mine = jnp.where(here, g[:, 192 * s : 192 * s + 192].astype(F32), mine)
        start = pl.multiple_of(block_start(me, r) + STEP, STEP)
        slab[pl.ds(start, ROWS), :] = mine.astype(BF16)
    for t in range(TAPS):
        first = (2 - t) * STEP
        shifted[:, 192 * t : 192 * t + 192] = slab[first : first + 512, :]
    result = dot(acted_ref[STEP : STEP + 512, :], shifted[...], TN)
    rows = 768 // parts
    half = rows // 2
    for j in range(parts):
        total[j] = result[j * rows : (j + 1) * rows]
    for n, out in enumerate(outs):
        piece = total[lax.rem(mx + n, parts)]
        out[...] = jnp.concatenate([piece[:half], piece[half:]], axis=1).astype(BF16)


def backward_kernel(ids, *refs):
    q, k, v = refs[0:4], refs[4:8], refs[8:12]
    g_whole, g_need, g_rest = refs[12:14], refs[14:16], refs[16:18]
    soft_ref, attended_ref, acted_ref, w_ref = refs[18:22]
    conv_ref, dq_ref, dk_ref, dv_ref = refs[22:26]
    km, vm, qm, g_pad, ga_ref, do_ref, dp_ref, ds_ref = refs[26:]
    me = ids[0]
    inverse = 1.0 / math.sqrt(HEAD_DIM)
    own = pl.multiple_of(me * ROWS, ROWS)
    conv = jnp.zeros((ROWS, 768), F32)
    for t in range(TAPS):
        rows = acted_ref[pl.ds(pl.multiple_of(own + t * STEP, STEP), ROWS), :]
        conv = conv + dot(rows, w_ref[t])
    conv_ref[...] = conv.astype(BF16)
    g_pad[0:STEP, :] = jnp.zeros((STEP, 768), BF16)
    g_pad[STEP + 512 :, :] = jnp.zeros((STEP, 768), BF16)
    for r in range(4):
        at = slice(r * ROWS, (r + 1) * ROWS)
        start = pl.multiple_of(block_start(me, r) + STEP, STEP)
        if r < 2:
            g_pad[pl.ds(start, ROWS), :] = g_whole[r][...]
        else:
            side = lax.div(me, 2)
            need = pl.ds(pl.multiple_of(side * 384, 128), 384)
            rest = pl.ds(pl.multiple_of((1 - side) * 384, 128), 384)
            g_pad[pl.ds(start, ROWS), need] = g_need[r - 2][...]
            g_pad[pl.ds(start, ROWS), rest] = g_rest[r - 2][...]
        for h in range(HEADS):
            km[h, at, :] = masked_window(window(k[r], h), h)
            vm[h, at, :] = masked_window(window(v[r], h), h)
            qm[h, at, :] = masked_window(window(q[r], h), h)
    ga_ref[...] = dot(g_pad[2 * STEP : 2 * STEP + 512, :], w_ref[0], NT)
    ga_ref[...] += dot(g_pad[STEP : STEP + 512, :], w_ref[1], NT)
    ga_ref[...] += dot(g_pad[0:512, :], w_ref[2], NT)
    for r in range(4):
        at = slice(r * ROWS, (r + 1) * ROWS)
        full = attended_ref[at, :].astype(F32)
        factor = lax.rsqrt(jnp.mean(full * full, axis=1, keepdims=True) + norm_epsilon)
        normed = full * factor
        grad = ga_ref[pl.ds(block_start(me, r), ROWS), :] * gelu_slope(normed)
        inner = jnp.mean(grad * normed, axis=1, keepdims=True)
        do_ref[at, :] = (factor * (grad - normed * inner)).astype(BF16)
    dq, dk, dv = [], [], []
    for h in range(HEADS):
        grad_out = window(do_ref, h)
        dp_ref[...] = dot(grad_out, vm[h], NT)
        for c in range(8):
            at = slice(c * 64, (c + 1) * 64)
            p = soft_ref[h, at, :]
            dp = dp_ref[at, :]
            inner = jnp.sum(dp * p, axis=1, keepdims=True)
            wide = 512 if c < 2 else ROWS
            ds_ref[at, 0:wide] = (p[:, :wide] * (dp[:, :wide] - inner) * inverse).astype(BF16)
        dq.append(dot(ds_ref[0:ROWS, :], km[h]))
        dk.append(dot(ds_ref[:, 0:ROWS], qm[h], TN))
        dv.append(dot(soft_ref[h, :, 0:ROWS].astype(BF16), masked_window(grad_out, h), TN))
    dq_ref[...] = place(dq).astype(BF16)
    dk_ref[...] = place(dk).astype(BF16)
    dv_ref[...] = place(dv).astype(BF16)


def sum_kernel(ids, *refs):
    parts, outs, total = refs[: ids_parts(refs)], refs[ids_parts(refs) : -1], refs[-1]
    mz = ids[2]
    value = parts[0][...].astype(F32)
    for part in parts[1:]:
        value = value + part[...].astype(F32)
    count = len(outs)
    rows = value.shape[0] // count
    for j in range(count):
        total[j, 0:rows, :] = value[j * rows : (j + 1) * rows]
    for n, out in enumerate(outs):
        out[...] = total[lax.rem(mz + n, count), 0:rows, :]


def ids_parts(refs):
    shape = refs[0].shape
    count = 0
    while refs[count].shape == shape and count < len(refs) - 1:
        count += 1
    return count


def half_kernel(ids, *refs):
    parts, (keep_ref, send_ref) = refs[:-2], refs[-2:]
    my = ids[3]
    value = parts[0][...].astype(F32)
    for part in parts[1:]:
        value = value + part[...].astype(F32)
    low, high = value[:, :576], value[:, 576:]
    keep_ref[...] = jnp.where(my == 0, low, high)
    send_ref[...] = jnp.where(my == 0, high, low).astype(BF16)


def last_kernel(scale, keep_ref, got_ref, out_ref):
    value = (keep_ref[...] + got_ref[...].astype(F32)) * scale
    for t in range(TAPS):
        out_ref[:, t, :] = value[:, 192 * t : 192 * t + 192]


def call(kernel, outs, scratch, args, flops, limit=24, in_hbm=()):
    size = sum(math.prod(a.shape) * a.dtype.itemsize for a in (*args, *outs))
    run = pl.pallas_call(
        kernel,
        out_shape=outs,
        in_specs=[
            pl.BlockSpec(
                memory_space=pltpu.SMEM
                if a.dtype == jnp.int32
                else pltpu.HBM
                if n in in_hbm
                else pltpu.VMEM
            )
            for n, a in enumerate(args)
        ],
        out_specs=[pl.BlockSpec(memory_space=pltpu.VMEM) for _ in outs],
        scratch_shapes=scratch,
        compiler_params=pltpu.CompilerParams(vmem_limit_bytes=limit << 20),
        cost_estimate=pl.CostEstimate(
            flops=flops, bytes_accessed=size, transcendentals=0
        ),
    )
    args = [
        pltpu.with_memory_space_constraint(a, pltpu.HBM) if n in in_hbm else a
        for n, a in enumerate(args)
    ]
    return run(*args)


def shaped(shape, dtype=BF16):
    return jax.ShapeDtypeStruct(shape, dtype)


def shift(value, axis, by):
    count = lax.axis_size(axis)
    return lax.ppermute(value, axis, [(i, (i + by) % count) for i in range(count)])


def ring(terms, axis):
    count = len(terms)
    right, left = count // 2, count - 1 - count // 2
    ahead = behind = None
    for step in range(right):
        n = right - step
        ahead = terms[n] if step == 0 else terms[n] + ahead.astype(F32)
        ahead = shift(ahead.astype(BF16), axis, 1)
        if step < left:
            n = count - left + step
            behind = terms[n] if step == 0 else terms[n] + behind.astype(F32)
            behind = shift(behind.astype(BF16), axis, -1)
    return [terms[0], ahead] + ([behind] if left else [])


def body(queries, key_rows, value_rows, conv_weight, output_gradient):
    x_size, z_size = lax.axis_size("x"), lax.axis_size("z")
    sizes = [lax.axis_size(a) for a in ("x", "yh", "z", "yl", "core")]
    grad_scale = 1.0 / math.sqrt(math.prod(sizes) * ROWS)
    me = lax.axis_index("yl") * 2 + lax.axis_index("core")
    ids = jnp.stack(
        [me, lax.axis_index("x"), lax.axis_index("z"), lax.axis_index("yh")]
    ).astype(jnp.int32)
    weight = jnp.transpose(conv_weight, (1, 0, 2))
    k, q, v, g = key_rows[0], queries[0], value_rows[0], output_gradient[0]
    half = 384
    side = lax.axis_index("yl")
    sent = {
        "k": k,
        "q": q,
        "v": v,
        "need": lax.dynamic_slice(g, (0, (1 - side) * half), (ROWS, half)),
        "rest": lax.dynamic_slice(g, (0, side * half), (ROWS, half)),
    }
    across = {n: shift(a, "yl", 1) for n, a in sent.items()}
    near = {n: shift(a, "core", 1) for n, a in (("k", k), ("q", q), ("v", v), ("g", g))}
    diag = {n: shift(a, "core", 1) for n, a in across.items()}
    q = (q, near["q"], across["q"], diag["q"])
    k = (k, near["k"], across["k"], diag["k"])
    v = (v, near["v"], across["v"], diag["v"])
    whole = (g, near["g"])
    need = (across["need"], diag["need"])
    rest = (across["rest"], diag["rest"])
    soft, attended, acted = call(
        forward_kernel,
        [shaped((HEADS, 512, 512), F32), shaped((512, 768)), shaped((576, 768))],
        [
            pltpu.VMEM((512, 768), BF16),
            pltpu.VMEM((HEADS, 512, 256), BF16),
            pltpu.VMEM((HEADS, 512, 256), BF16),
            pltpu.VMEM((512, 512), F32),
            pltpu.VMEM((512, 512), BF16),
            pltpu.VMEM((HEADS, 512, 256), F32),
            pltpu.VMEM((3, ROWS, 768), BF16),
            pltpu.SemaphoreType.DMA((3,)),
        ],
        [ids, *q, *k, *v],
        2_000_000_000,
        in_hbm=(1, 5, 9),
    )
    rows = 768 // x_size
    pieces = call(
        weight_kernel,
        [shaped((rows // 2, 1152)) for _ in range(x_size)],
        [
            pltpu.VMEM((576, HEAD_DIM), BF16),
            pltpu.VMEM((512, 576), BF16),
            pltpu.VMEM((x_size, rows, 576), F32),
        ],
        [ids, acted, *whole, *need],
        500_000_000,
    )
    got = [pieces[0]] + [shift(pieces[n], "x", n) for n in range(1, x_size)]
    conv_out, grad_queries, grad_keys, grad_values = call(
        backward_kernel,
        [shaped((ROWS, 768)) for _ in range(4)],
        [
            pltpu.VMEM((HEADS, 512, 256), BF16),
            pltpu.VMEM((HEADS, 512, 256), BF16),
            pltpu.VMEM((HEADS, 512, 256), BF16),
            pltpu.VMEM((576, 768), BF16),
            pltpu.VMEM((512, 768), F32),
            pltpu.VMEM((512, 768), BF16),
            pltpu.VMEM((512, 512), F32),
            pltpu.VMEM((512, 512), BF16),
        ],
        [ids, *q, *k, *v, *whole, *need, *rest, soft, attended, acted, weight],
        4_000_000_000,
        36,
    )
    few = rows // 2 // z_size
    pieces = call(
        sum_kernel,
        [shaped((few, 1152), F32) for _ in range(z_size)],
        [pltpu.VMEM((z_size, -(-few // 8) * 8, 1152), F32)],
        [ids, *got],
        1_000_000,
    )
    got = ring(pieces, "z")
    keep, send = call(
        half_kernel, [shaped((few, 576), F32), shaped((few, 576))], [], [ids, *got], 1_000_000
    )
    other = shift(send, "yh", 1)
    (grad_weight,) = call(
        lambda *refs: last_kernel(grad_scale, *refs),
        [shaped((few, TAPS, HEAD_DIM), F32)],
        [],
        [keep, other],
        1_000_000,
    )
    return conv_out[None], grad_queries[None], grad_keys[None], grad_values[None], grad_weight


def solution(mesh):
    x, yh, z = SPLITS[mesh.shape["dp"]]
    fine = Mesh(mesh.devices.reshape(x, yh, z, 2, 2), ("x", "yh", "z", "yl", "core"))
    dp, seq = ("x", "yh", "z"), ("yl", "core")
    return jax.shard_map(
        body,
        mesh=fine,
        in_specs=(P(dp, seq, None), P(dp, seq, None), P(dp, seq, None), P(), P(dp, seq, None)),
        out_specs=(
            P(dp, seq, None),
            P(dp, seq, None),
            P(dp, seq, None),
            P(dp, seq, None),
            P(dp, None, seq),
        ),
        check_vma=False,
    )
```

```python
import math

import jax
import jax.numpy as jnp
from jax import lax
from jax.experimental import pallas as pl
from jax.experimental.pallas import tpu as pltpu
from jax.sharding import Mesh, PartitionSpec as P


HEADS = 4
HEAD_DIM = 192
TAPS = 3
STEP = 32
ROWS = 128
SPLITS = {64: (4, 2, 8), 16: (1, 2, 8)}

tanh_scale = 0.7978845608028654
cubic_term = 0.044715
norm_epsilon = 1e-06

F32 = jnp.float32
BF16 = jnp.bfloat16
WINDOW = (0, 128, 384, 512)
FIRST = (0, 64, 0, 64)
NT = (((1,), (1,)), ((), ()))
TN = (((0,), (0,)), ((), ()))


def dot(a, b, dims=(((1,), (0,)), ((), ()))):
    return lax.dot_general(a, b, dims, preferred_element_type=F32)


def masked_window(value, head):
    lane = lax.broadcasted_iota(jnp.int32, value.shape, 1)
    first = FIRST[head]
    keep = (lane >= first) & (lane < first + HEAD_DIM)
    return jnp.where(keep, value, jnp.zeros_like(value))


def window(ref, head):
    return ref[:, WINDOW[head] : WINDOW[head] + 256]


def place(parts):
    a, b, c, d = parts
    return jnp.concatenate(
        [
            a[:, :128],
            a[:, 128:] + b[:, :128],
            b[:, 128:],
            c[:, :128],
            c[:, 128:] + d[:, :128],
            d[:, 128:],
        ],
        axis=1,
    )


def gelu_value(value):
    inner = tanh_scale * (value + cubic_term * value * value * value)
    return 0.5 * value * (1.0 + jnp.tanh(inner))


def gelu_slope(value):
    square = value * value
    tangent = jnp.tanh(tanh_scale * (value + cubic_term * square * value))
    return 0.5 * (1.0 + tangent) + 0.5 * value * (1.0 - tangent * tangent) * tanh_scale * (
        1.0 + 3.0 * cubic_term * square
    )


def block_start(me, relative):
    return pl.multiple_of(jnp.bitwise_xor(me, relative) * ROWS, ROWS)


def score_kernel(ids, *refs):
    q, k, own_v = refs[0:4], refs[4:8], refs[8]
    soft_ref, rounded_ref, v_ref = refs[9:12]
    q_all, km, s_ref, own, sems = refs[12:]
    inverse = 1.0 / math.sqrt(HEAD_DIM)
    copies = [
        pltpu.make_async_copy(source, target, sems.at[n])
        for n, (source, target) in enumerate(
            ((q[0], own.at[0]), (k[0], own.at[1]), (own_v, v_ref))
        )
    ]
    for copy in copies:
        copy.start()
    for r in (1, 2, 3, 0):
        at = slice(r * ROWS, (r + 1) * ROWS)
        if r == 0:
            for copy in copies:
                copy.wait()
        q_all[at, :] = own[0] if r == 0 else q[r][...]
        for h in range(HEADS):
            km[h, at, :] = masked_window(window(own.at[1] if r == 0 else k[r], h), h)
    for h in range(HEADS):
        s_ref[...] = dot(window(q_all, h), km[h], NT)
        for c in range(8):
            at = slice(c * 64, (c + 1) * 64)
            s = s_ref[at, :] * inverse
            e = jnp.exp(s - jnp.max(s, axis=1, keepdims=True))
            p = e / jnp.sum(e, axis=1, keepdims=True)
            soft_ref[h, at, :] = p
            rounded_ref[h, at, :] = p.astype(BF16)


def attend_kernel(ids, *refs):
    rounded_ref, v = refs[0], refs[1:5]
    attended_ref, acted_ref = refs[5:7]
    vm, o_ref = refs[7:]
    me = ids[0]
    for r in range(4):
        at = slice(r * ROWS, (r + 1) * ROWS)
        for h in range(HEADS):
            vm[h, at, :] = masked_window(window(v[r], h), h)
    for h in range(HEADS):
        o_ref[h] = dot(rounded_ref[h], vm[h])
    acted_ref[0:STEP, :] = jnp.zeros((STEP, 768), BF16)
    acted_ref[STEP + 512 :, :] = jnp.zeros((STEP, 768), BF16)
    for r in range(4):
        at = slice(r * ROWS, (r + 1) * ROWS)
        attended = place([o_ref[h, at, :] for h in range(HEADS)]).astype(BF16)
        attended_ref[at, :] = attended
        full = attended.astype(F32)
        factor = lax.rsqrt(jnp.mean(full * full, axis=1, keepdims=True) + norm_epsilon)
        start = pl.multiple_of(block_start(me, r) + STEP, STEP)
        acted_ref[pl.ds(start, ROWS), :] = gelu_value(full * factor).astype(BF16)


def weight_kernel(ids, acted_ref, g_own, g_core, g_across, g_diag, *refs):
    outs, (slab, shifted, total) = refs[:-3], refs[-3:]
    me, mx = ids[0], ids[1]
    parts = len(outs)
    slab[0:STEP, :] = jnp.zeros((STEP, HEAD_DIM), BF16)
    slab[STEP + 512 :, :] = jnp.zeros((STEP, HEAD_DIM), BF16)
    for r, g in enumerate((g_own, g_core, g_across, g_diag)):
        mine = g[:, 0:192].astype(F32)
        count = g.shape[1] // HEAD_DIM
        for s in range(1, count):
            here = lax.rem(me, count) == s
            mine = jnp.where(here, g[:, 192 * s : 192 * s + 192].astype(F32), mine)
        start = pl.multiple_of(block_start(me, r) + STEP, STEP)
        slab[pl.ds(start, ROWS), :] = mine.astype(BF16)
    for t in range(TAPS):
        first = (2 - t) * STEP
        shifted[:, 192 * t : 192 * t + 192] = slab[first : first + 512, :]
    result = dot(acted_ref[STEP : STEP + 512, :], shifted[...], TN)
    rows = 768 // parts
    half = rows // 2
    for j in range(parts):
        total[j] = result[j * rows : (j + 1) * rows]
    for n, out in enumerate(outs):
        piece = total[jnp.bitwise_xor(mx, n)]
        out[...] = jnp.concatenate([piece[:half], piece[half:]], axis=1).astype(BF16)


def backward_kernel(ids, *refs):
    q, k, v = refs[0:4], refs[4:8], refs[8:12]
    g_whole, g_need, g_rest = refs[12:14], refs[14:16], refs[16:18]
    soft_ref, attended_ref, acted_ref, w_ref = refs[18:22]
    conv_ref, dq_ref, dk_ref, dv_ref = refs[22:26]
    km, vm, qm, g_pad, ga_ref, do_ref, dp_ref, ds_ref = refs[26:]
    me = ids[0]
    inverse = 1.0 / math.sqrt(HEAD_DIM)
    own = pl.multiple_of(me * ROWS, ROWS)
    conv = jnp.zeros((ROWS, 768), F32)
    for t in range(TAPS):
        rows = acted_ref[pl.ds(pl.multiple_of(own + t * STEP, STEP), ROWS), :]
        conv = conv + dot(rows, w_ref[t])
    conv_ref[...] = conv.astype(BF16)
    g_pad[0:STEP, :] = jnp.zeros((STEP, 768), BF16)
    g_pad[STEP + 512 :, :] = jnp.zeros((STEP, 768), BF16)
    for r in range(4):
        at = slice(r * ROWS, (r + 1) * ROWS)
        start = pl.multiple_of(block_start(me, r) + STEP, STEP)
        if r < 2:
            g_pad[pl.ds(start, ROWS), :] = g_whole[r][...]
        else:
            side = lax.div(me, 2)
            need = pl.ds(pl.multiple_of(side * 384, 128), 384)
            rest = pl.ds(pl.multiple_of((1 - side) * 384, 128), 384)
            g_pad[pl.ds(start, ROWS), need] = g_need[r - 2][...]
            g_pad[pl.ds(start, ROWS), rest] = g_rest[r - 2][...]
        for h in range(HEADS):
            km[h, at, :] = masked_window(window(k[r], h), h)
            vm[h, at, :] = masked_window(window(v[r], h), h)
            qm[h, at, :] = masked_window(window(q[r], h), h)
    ga_ref[...] = dot(g_pad[2 * STEP : 2 * STEP + 512, :], w_ref[0], NT)
    ga_ref[...] += dot(g_pad[STEP : STEP + 512, :], w_ref[1], NT)
    ga_ref[...] += dot(g_pad[0:512, :], w_ref[2], NT)
    for r in range(4):
        at = slice(r * ROWS, (r + 1) * ROWS)
        full = attended_ref[at, :].astype(F32)
        factor = lax.rsqrt(jnp.mean(full * full, axis=1, keepdims=True) + norm_epsilon)
        normed = full * factor
        grad = ga_ref[pl.ds(block_start(me, r), ROWS), :] * gelu_slope(normed)
        inner = jnp.mean(grad * normed, axis=1, keepdims=True)
        do_ref[at, :] = (factor * (grad - normed * inner)).astype(BF16)
    dq, dk, dv = [], [], []
    for h in range(HEADS):
        grad_out = window(do_ref, h)
        dp_ref[...] = dot(grad_out, vm[h], NT)
        for c in range(8):
            at = slice(c * 64, (c + 1) * 64)
            p = soft_ref[h, at, :]
            dp = dp_ref[at, :]
            inner = jnp.sum(dp * p, axis=1, keepdims=True)
            wide = 512 if c < 2 else ROWS
            ds_ref[at, 0:wide] = (p[:, :wide] * (dp[:, :wide] - inner) * inverse).astype(BF16)
        dq.append(dot(ds_ref[0:ROWS, :], km[h]))
        dk.append(dot(ds_ref[:, 0:ROWS], qm[h], TN))
        dv.append(dot(soft_ref[h, :, 0:ROWS].astype(BF16), masked_window(grad_out, h), TN))
    dq_ref[...] = place(dq).astype(BF16)
    dk_ref[...] = place(dk).astype(BF16)
    dv_ref[...] = place(dv).astype(BF16)


def total_of(parts):
    value = parts[0][...].astype(F32)
    for part in parts[1:]:
        value = value + part[...].astype(F32)
    return value


def near_kernel(ids, *refs):
    parts, outs, total = refs[:-5], refs[-5:-1], refs[-1]
    low = lax.rem(ids[2], 4)
    value = total_of(parts)
    few = value.shape[0] // 8
    for j in range(4):
        for high in range(2):
            at = (4 * high + j) * few
            total[j, high * few : (high + 1) * few, :] = value[at : at + few]
    for n, out in enumerate(outs):
        out[...] = total[jnp.bitwise_xor(low, n)].astype(out.dtype)


def far_kernel(ids, *refs):
    parts, outs = refs[:-4], refs[-4:]
    high, my = lax.div(ids[2], 4), ids[3]
    value = total_of(parts)
    few, wide = value.shape[0] // 2, value.shape[1] // 2
    rows = (value[:few], value[few:])
    for n, out in enumerate(outs):
        piece = jnp.where(high == n // 2, rows[0], rows[1])
        piece = jnp.where(my == n % 2, piece[:, :wide], piece[:, wide:])
        out[...] = piece.astype(out.dtype)


def last_kernel(scale, *refs):
    value = total_of(refs[:-1]) * scale
    for t in range(TAPS):
        refs[-1][:, t, :] = value[:, 192 * t : 192 * t + 192]


def call(kernel, outs, scratch, args, flops, limit=16, in_hbm=()):
    size = sum(math.prod(a.shape) * a.dtype.itemsize for a in (*args, *outs))
    run = pl.pallas_call(
        kernel,
        out_shape=outs,
        in_specs=[
            pl.BlockSpec(
                memory_space=pltpu.SMEM
                if a.dtype == jnp.int32
                else pltpu.HBM
                if n in in_hbm
                else pltpu.VMEM
            )
            for n, a in enumerate(args)
        ],
        out_specs=[pl.BlockSpec(memory_space=pltpu.VMEM) for _ in outs],
        scratch_shapes=scratch,
        compiler_params=pltpu.CompilerParams(vmem_limit_bytes=limit << 20),
        cost_estimate=pl.CostEstimate(
            flops=flops, bytes_accessed=size, transcendentals=0
        ),
    )
    args = [
        pltpu.with_memory_space_constraint(a, pltpu.HBM) if n in in_hbm else a
        for n, a in enumerate(args)
    ]
    return run(*args)


def shaped(shape, dtype=BF16):
    return jax.ShapeDtypeStruct(shape, dtype)


def swap(value, axis, mask):
    count = lax.axis_size(axis)
    return lax.ppermute(value, axis, [(i, i ^ mask) for i in range(count)])


def body(queries, key_rows, value_rows, conv_weight, output_gradient):
    x_size = lax.axis_size("x")
    sizes = [lax.axis_size(a) for a in ("x", "yh", "z", "yl", "core")]
    grad_scale = 1.0 / math.sqrt(math.prod(sizes) * ROWS)
    me = lax.axis_index("yl") * 2 + lax.axis_index("core")
    ids = jnp.stack(
        [me, lax.axis_index("x"), lax.axis_index("z"), lax.axis_index("yh")]
    ).astype(jnp.int32)
    weight = jnp.transpose(conv_weight, (1, 0, 2))
    k, q, v, g = key_rows[0], queries[0], value_rows[0], output_gradient[0]
    half = 384
    side = lax.axis_index("yl")
    sent = {
        "k": k,
        "q": q,
        "v": v,
        "need": lax.dynamic_slice(g, (0, (1 - side) * half), (ROWS, half)),
        "rest": lax.dynamic_slice(g, (0, side * half), (ROWS, half)),
    }
    across = {n: swap(a, "yl", 1) for n, a in sent.items()}
    near = {n: swap(a, "core", 1) for n, a in (("k", k), ("q", q), ("v", v), ("g", g))}
    diag = {n: swap(a, "core", 1) for n, a in across.items()}
    q = (q, near["q"], across["q"], diag["q"])
    k = (k, near["k"], across["k"], diag["k"])
    v = (v, near["v"], across["v"], diag["v"])
    whole = (g, near["g"])
    need = (across["need"], diag["need"])
    rest = (across["rest"], diag["rest"])
    soft, rounded, own_v = call(
        score_kernel,
        [
            shaped((HEADS, 512, 512), F32),
            shaped((HEADS, 512, 512)),
            shaped((ROWS, 768)),
        ],
        [
            pltpu.VMEM((512, 768), BF16),
            pltpu.VMEM((HEADS, 512, 256), BF16),
            pltpu.VMEM((512, 512), F32),
            pltpu.VMEM((2, ROWS, 768), BF16),
            pltpu.SemaphoreType.DMA((3,)),
        ],
        [ids, *q, *k, v[0]],
        1_000_000_000,
        in_hbm=(1, 5, 9),
    )
    v = (own_v, *v[1:])
    attended, acted = call(
        attend_kernel,
        [shaped((512, 768)), shaped((576, 768))],
        [pltpu.VMEM((HEADS, 512, 256), BF16), pltpu.VMEM((HEADS, 512, 256), F32)],
        [ids, rounded, *v],
        1_000_000_000,
    )
    rows = 768 // x_size
    pieces = call(
        weight_kernel,
        [shaped((rows // 2, 1152)) for _ in range(x_size)],
        [
            pltpu.VMEM((576, HEAD_DIM), BF16),
            pltpu.VMEM((512, 576), BF16),
            pltpu.VMEM((x_size, rows, 576), F32),
        ],
        [ids, acted, *whole, *need],
        500_000_000,
    )
    got = [pieces[0]] + [swap(pieces[n], "x", n) for n in range(1, x_size)]
    conv_out, grad_queries, grad_keys, grad_values = call(
        backward_kernel,
        [shaped((ROWS, 768)) for _ in range(4)],
        [
            pltpu.VMEM((HEADS, 512, 256), BF16),
            pltpu.VMEM((HEADS, 512, 256), BF16),
            pltpu.VMEM((HEADS, 512, 256), BF16),
            pltpu.VMEM((576, 768), BF16),
            pltpu.VMEM((512, 768), F32),
            pltpu.VMEM((512, 768), BF16),
            pltpu.VMEM((512, 512), F32),
            pltpu.VMEM((512, 512), BF16),
        ],
        [ids, *q, *k, *v, *whole, *need, *rest, soft, attended, acted, weight],
        4_000_000_000,
        24,
    )
    few = rows // 16
    pieces = call(
        near_kernel,
        [shaped((2 * few, 1152), F32)] + [shaped((2 * few, 1152)) for _ in range(3)],
        [pltpu.VMEM((4, 2 * few, 1152), F32)],
        [ids, *got],
        1_000_000,
    )
    got = [pieces[0]] + [swap(pieces[n], "z", n) for n in range(1, 4)]
    pieces = call(
        far_kernel,
        [shaped((few, 576), F32)] + [shaped((few, 576)) for _ in range(3)],
        [],
        [ids, *got],
        1_000_000,
    )
    got = [pieces[0]] + [swap(pieces[1], "yh", 1), swap(pieces[2], "z", 4)]
    got.append(swap(pieces[3], ("yh", "z"), 12))
    (grad_weight,) = call(
        lambda *refs: last_kernel(grad_scale, *refs),
        [shaped((few, TAPS, HEAD_DIM), F32)],
        [],
        got,
        1_000_000,
    )
    return conv_out[None], grad_queries[None], grad_keys[None], grad_values[None], grad_weight


def solution(mesh):
    x, yh, z = SPLITS[mesh.shape["dp"]]
    fine = Mesh(mesh.devices.reshape(x, yh, z, 2, 2), ("x", "yh", "z", "yl", "core"))
    dp, seq = ("x", "yh", "z"), ("yl", "core")
    return jax.shard_map(
        body,
        mesh=fine,
        in_specs=(P(dp, seq, None), P(dp, seq, None), P(dp, seq, None), P(), P(dp, seq, None)),
        out_specs=(
            P(dp, seq, None),
            P(dp, seq, None),
            P(dp, seq, None),
            P(dp, seq, None),
            P(dp, None, seq),
        ),
        check_vma=False,
    )
```

```python
import math

import jax
import jax.numpy as jnp
from jax import lax
from jax.experimental import pallas as pl
from jax.experimental.pallas import tpu as pltpu
from jax.sharding import Mesh, PartitionSpec as P


HEADS = 4
HEAD_DIM = 192
TAPS = 3
STEP = 32
ROWS = 128
SPLITS = {64: (4, 2, 8), 16: (1, 2, 8)}

tanh_scale = 0.7978845608028654
cubic_term = 0.044715
norm_epsilon = 1e-06

F32 = jnp.float32
BF16 = jnp.bfloat16
WINDOW = (0, 128, 384, 512)
FIRST = (0, 64, 0, 64)
NT = (((1,), (1,)), ((), ()))
TN = (((0,), (0,)), ((), ()))


def dot(a, b, dims=(((1,), (0,)), ((), ()))):
    return lax.dot_general(a, b, dims, preferred_element_type=F32)


def masked_window(value, head):
    lane = lax.broadcasted_iota(jnp.int32, value.shape, 1)
    first = FIRST[head]
    keep = (lane >= first) & (lane < first + HEAD_DIM)
    return jnp.where(keep, value, jnp.zeros_like(value))


def window(ref, head):
    return ref[:, WINDOW[head] : WINDOW[head] + 256]


def place(parts):
    a, b, c, d = parts
    return jnp.concatenate(
        [
            a[:, :128],
            a[:, 128:] + b[:, :128],
            b[:, 128:],
            c[:, :128],
            c[:, 128:] + d[:, :128],
            d[:, 128:],
        ],
        axis=1,
    )


def gelu_value(value):
    inner = tanh_scale * (value + cubic_term * value * value * value)
    return 0.5 * value * (1.0 + jnp.tanh(inner))


def gelu_slope(value):
    square = value * value
    tangent = jnp.tanh(tanh_scale * (value + cubic_term * square * value))
    return 0.5 * (1.0 + tangent) + 0.5 * value * (1.0 - tangent * tangent) * tanh_scale * (
        1.0 + 3.0 * cubic_term * square
    )


def block_start(me, relative):
    return pl.multiple_of(jnp.bitwise_xor(me, relative) * ROWS, ROWS)


def prep_kernel(ids, *refs):
    sources, owns, (need_ref, rest_ref), sems = refs[:4], refs[4:8], refs[8:10], refs[10]
    copies = [
        pltpu.make_async_copy(source, own, sems.at[n])
        for n, (source, own) in enumerate(zip(sources, owns))
    ]
    for copy in copies:
        copy.start()
    for copy in copies:
        copy.wait()
    side = lax.div(ids[0], 2)
    need = pl.multiple_of((1 - side) * 384, 128)
    rest = pl.multiple_of(side * 384, 128)
    need_ref[...] = owns[3][:, pl.ds(need, 384)]
    rest_ref[...] = owns[3][:, pl.ds(rest, 384)]


def keys_kernel(*refs):
    k, km = refs[:4], refs[4]
    for r in range(4):
        at = slice(r * ROWS, (r + 1) * ROWS)
        for h in range(HEADS):
            km[h, at, :] = masked_window(window(k[r], h), h)


def score_kernel(*refs):
    q, km = refs[0:4], refs[4]
    soft_ref, rounded_ref = refs[5:7]
    q_all, s_ref = refs[7:]
    inverse = 1.0 / math.sqrt(HEAD_DIM)
    for r in range(4):
        q_all[r * ROWS : (r + 1) * ROWS, :] = q[r][...]
    for h in range(HEADS):
        s_ref[...] = dot(window(q_all, h), km[h], NT)
        for c in range(8):
            at = slice(c * 64, (c + 1) * 64)
            s = s_ref[at, :] * inverse
            e = jnp.exp(s - jnp.max(s, axis=1, keepdims=True))
            p = e / jnp.sum(e, axis=1, keepdims=True)
            soft_ref[h, at, :] = p
            rounded_ref[h, at, :] = p.astype(BF16)


def attend_kernel(ids, *refs):
    rounded_ref, v = refs[0], refs[1:5]
    attended_ref, acted_ref, vm = refs[5:8]
    o_ref = refs[8]
    me = ids[0]
    for r in range(4):
        at = slice(r * ROWS, (r + 1) * ROWS)
        for h in range(HEADS):
            vm[h, at, :] = masked_window(window(v[r], h), h)
    for h in range(HEADS):
        o_ref[h] = dot(rounded_ref[h], vm[h])
    acted_ref[0:STEP, :] = jnp.zeros((STEP, 768), BF16)
    acted_ref[STEP + 512 :, :] = jnp.zeros((STEP, 768), BF16)
    for r in range(4):
        at = slice(r * ROWS, (r + 1) * ROWS)
        attended = place([o_ref[h, at, :] for h in range(HEADS)]).astype(BF16)
        attended_ref[at, :] = attended
        full = attended.astype(F32)
        factor = lax.rsqrt(jnp.mean(full * full, axis=1, keepdims=True) + norm_epsilon)
        start = pl.multiple_of(block_start(me, r) + STEP, STEP)
        acted_ref[pl.ds(start, ROWS), :] = gelu_value(full * factor).astype(BF16)


def weight_kernel(ids, acted_ref, g_own, g_core, g_across, g_diag, *refs):
    outs, (slab, shifted, total) = refs[:-3], refs[-3:]
    me, mx = ids[0], ids[1]
    parts = len(outs)
    slab[0:STEP, :] = jnp.zeros((STEP, HEAD_DIM), BF16)
    slab[STEP + 512 :, :] = jnp.zeros((STEP, HEAD_DIM), BF16)
    for r, g in enumerate((g_own, g_core, g_across, g_diag)):
        mine = g[:, 0:192].astype(F32)
        count = g.shape[1] // HEAD_DIM
        for s in range(1, count):
            here = lax.rem(me, count) == s
            mine = jnp.where(here, g[:, 192 * s : 192 * s + 192].astype(F32), mine)
        start = pl.multiple_of(block_start(me, r) + STEP, STEP)
        slab[pl.ds(start, ROWS), :] = mine.astype(BF16)
    for t in range(TAPS):
        first = (2 - t) * STEP
        shifted[:, 192 * t : 192 * t + 192] = slab[first : first + 512, :]
    result = dot(acted_ref[STEP : STEP + 512, :], shifted[...], TN)
    rows = 768 // parts
    half = rows // 2
    for j in range(parts):
        total[j] = result[j * rows : (j + 1) * rows]
    for n, out in enumerate(outs):
        piece = total[jnp.bitwise_xor(mx, n)]
        out[...] = jnp.concatenate([piece[:half], piece[half:]], axis=1).astype(BF16)


def backward_kernel(ids, *refs):
    q, km, vm = refs[0:4], refs[4], refs[5]
    g_whole, g_need, g_rest = refs[6:8], refs[8:10], refs[10:12]
    soft_ref, attended_ref, acted_ref, w_ref = refs[12:16]
    conv_ref, dq_ref, dk_ref, dv_ref = refs[16:20]
    qm, g_pad, ga_ref, do_ref, dp_ref, ds_ref = refs[20:]
    me = ids[0]
    inverse = 1.0 / math.sqrt(HEAD_DIM)
    own = pl.multiple_of(me * ROWS, ROWS)
    conv = jnp.zeros((ROWS, 768), F32)
    for t in range(TAPS):
        rows = acted_ref[pl.ds(pl.multiple_of(own + t * STEP, STEP), ROWS), :]
        conv = conv + dot(rows, w_ref[t])
    conv_ref[...] = conv.astype(BF16)
    g_pad[0:STEP, :] = jnp.zeros((STEP, 768), BF16)
    g_pad[STEP + 512 :, :] = jnp.zeros((STEP, 768), BF16)
    for r in range(4):
        at = slice(r * ROWS, (r + 1) * ROWS)
        start = pl.multiple_of(block_start(me, r) + STEP, STEP)
        if r < 2:
            g_pad[pl.ds(start, ROWS), :] = g_whole[r][...]
        else:
            side = lax.div(me, 2)
            need = pl.ds(pl.multiple_of(side * 384, 128), 384)
            rest = pl.ds(pl.multiple_of((1 - side) * 384, 128), 384)
            g_pad[pl.ds(start, ROWS), need] = g_need[r - 2][...]
            g_pad[pl.ds(start, ROWS), rest] = g_rest[r - 2][...]
        for h in range(HEADS):
            qm[h, at, :] = masked_window(window(q[r], h), h)
    ga_ref[...] = dot(g_pad[2 * STEP : 2 * STEP + 512, :], w_ref[0], NT)
    ga_ref[...] += dot(g_pad[STEP : STEP + 512, :], w_ref[1], NT)
    ga_ref[...] += dot(g_pad[0:512, :], w_ref[2], NT)
    for r in range(4):
        at = slice(r * ROWS, (r + 1) * ROWS)
        full = attended_ref[at, :].astype(F32)
        factor = lax.rsqrt(jnp.mean(full * full, axis=1, keepdims=True) + norm_epsilon)
        normed = full * factor
        grad = ga_ref[pl.ds(block_start(me, r), ROWS), :] * gelu_slope(normed)
        inner = jnp.mean(grad * normed, axis=1, keepdims=True)
        do_ref[at, :] = (factor * (grad - normed * inner)).astype(BF16)
    dq, dk, dv = [], [], []
    for h in range(HEADS):
        grad_out = window(do_ref, h)
        dp_ref[...] = dot(grad_out, vm[h], NT)
        for c in range(8):
            at = slice(c * 64, (c + 1) * 64)
            p = soft_ref[h, at, :]
            dp = dp_ref[at, :]
            inner = jnp.sum(dp * p, axis=1, keepdims=True)
            wide = 512 if c < 2 else ROWS
            ds_ref[at, 0:wide] = (p[:, :wide] * (dp[:, :wide] - inner) * inverse).astype(BF16)
        dq.append(dot(ds_ref[0:ROWS, :], km[h]))
        dk.append(dot(ds_ref[:, 0:ROWS], qm[h], TN))
        dv.append(dot(soft_ref[h, :, 0:ROWS].astype(BF16), masked_window(grad_out, h), TN))
    dq_ref[...] = place(dq).astype(BF16)
    dk_ref[...] = place(dk).astype(BF16)
    dv_ref[...] = place(dv).astype(BF16)


def total_of(parts):
    value = parts[0][...].astype(F32)
    for part in parts[1:]:
        value = value + part[...].astype(F32)
    return value


def near_kernel(ids, *refs):
    parts, outs, total = refs[:-5], refs[-5:-1], refs[-1]
    pair = lax.div(ids[2], 2)
    value = total_of(parts)
    rows = value.shape[0] // 4
    for j in range(4):
        total[j] = value[j * rows : (j + 1) * rows]
    for n, out in enumerate(outs):
        out[...] = total[jnp.bitwise_xor(pair, n)].astype(out.dtype)


def far_kernel(ids, *refs):
    parts, outs = refs[:-4], refs[-4:]
    odd, my = lax.rem(ids[2], 2), ids[3]
    value = total_of(parts)
    few, wide = value.shape[0] // 2, value.shape[1] // 2
    rows = (value[:few], value[few:])
    for n, out in enumerate(outs):
        piece = jnp.where(odd == n // 2, rows[0], rows[1])
        piece = jnp.where(my == n % 2, piece[:, :wide], piece[:, wide:])
        out[...] = piece.astype(out.dtype)


def last_kernel(scale, *refs):
    value = total_of(refs[:-1]) * scale
    for t in range(TAPS):
        refs[-1][:, t, :] = value[:, 192 * t : 192 * t + 192]


def call(kernel, outs, scratch, args, flops, limit=16, in_hbm=()):
    size = sum(math.prod(a.shape) * a.dtype.itemsize for a in (*args, *outs))
    run = pl.pallas_call(
        kernel,
        out_shape=outs,
        in_specs=[
            pl.BlockSpec(
                memory_space=pltpu.SMEM
                if a.dtype == jnp.int32
                else pltpu.HBM
                if n in in_hbm
                else pltpu.VMEM
            )
            for n, a in enumerate(args)
        ],
        out_specs=[pl.BlockSpec(memory_space=pltpu.VMEM) for _ in outs],
        scratch_shapes=scratch,
        compiler_params=pltpu.CompilerParams(vmem_limit_bytes=limit << 20),
        cost_estimate=pl.CostEstimate(
            flops=flops, bytes_accessed=size, transcendentals=0
        ),
    )
    args = [
        pltpu.with_memory_space_constraint(a, pltpu.HBM) if n in in_hbm else a
        for n, a in enumerate(args)
    ]
    return run(*args)


def shaped(shape, dtype=BF16):
    return jax.ShapeDtypeStruct(shape, dtype)


def swap(value, axis, mask):
    count = lax.axis_size(axis)
    return lax.ppermute(value, axis, [(i, i ^ mask) for i in range(count)])


def body(queries, key_rows, value_rows, conv_weight, output_gradient):
    x_size = lax.axis_size("x")
    sizes = [lax.axis_size(a) for a in ("x", "yh", "z", "yl", "core")]
    grad_scale = 1.0 / math.sqrt(math.prod(sizes) * ROWS)
    me = lax.axis_index("yl") * 2 + lax.axis_index("core")
    ids = jnp.stack(
        [me, lax.axis_index("x"), lax.axis_index("z"), lax.axis_index("yh")]
    ).astype(jnp.int32)
    weight = jnp.transpose(conv_weight, (1, 0, 2))
    k, q, v, g = key_rows[0], queries[0], value_rows[0], output_gradient[0]
    first = {n: swap(a, "yl", 1) for n, a in (("k", k), ("q", q))}
    own_q, own_k, own_v, own_g, need, rest = call(
        prep_kernel,
        [shaped((ROWS, 768)) for _ in range(4)] + [shaped((ROWS, 384)) for _ in range(2)],
        [pltpu.SemaphoreType.DMA((4,))],
        [ids, q, k, v, g],
        1_000_000,
        in_hbm=(1, 2, 3, 4),
    )
    sent = {"v": v, "need": need, "rest": rest}
    across = first | {n: swap(a, "yl", 1) for n, a in sent.items()}
    near = {n: swap(a, "core", 1) for n, a in (("k", k), ("q", q), ("v", v), ("g", g))}
    diag = {n: swap(a, "core", 1) for n, a in across.items()}
    q = (own_q, near["q"], across["q"], diag["q"])
    k = (own_k, near["k"], across["k"], diag["k"])
    v = (own_v, near["v"], across["v"], diag["v"])
    whole = (own_g, near["g"])
    need = (across["need"], diag["need"])
    rest = (across["rest"], diag["rest"])
    (km,) = call(keys_kernel, [shaped((HEADS, 512, 256))], [], k, 1_000_000)
    soft, rounded = call(
        score_kernel,
        [shaped((HEADS, 512, 512), F32), shaped((HEADS, 512, 512))],
        [
            pltpu.VMEM((512, 768), BF16),
            pltpu.VMEM((512, 512), F32),
        ],
        [*q, km],
        1_000_000_000,
    )
    attended, acted, vm = call(
        attend_kernel,
        [shaped((512, 768)), shaped((576, 768)), shaped((HEADS, 512, 256))],
        [pltpu.VMEM((HEADS, 512, 256), F32)],
        [ids, rounded, *v],
        1_000_000_000,
    )
    rows = 768 // x_size
    pieces = call(
        weight_kernel,
        [shaped((rows // 2, 1152)) for _ in range(x_size)],
        [
            pltpu.VMEM((576, HEAD_DIM), BF16),
            pltpu.VMEM((512, 576), BF16),
            pltpu.VMEM((x_size, rows, 576), F32),
        ],
        [ids, acted, *whole, *need],
        500_000_000,
    )
    got = [pieces[0]] + [swap(pieces[n], "x", n) for n in range(1, x_size)]
    conv_out, grad_queries, grad_keys, grad_values = call(
        backward_kernel,
        [shaped((ROWS, 768)) for _ in range(4)],
        [
            pltpu.VMEM((HEADS, 512, 256), BF16),
            pltpu.VMEM((576, 768), BF16),
            pltpu.VMEM((512, 768), F32),
            pltpu.VMEM((512, 768), BF16),
            pltpu.VMEM((512, 512), F32),
            pltpu.VMEM((512, 512), BF16),
        ],
        [ids, *q, km, vm, *whole, *need, *rest, soft, attended, acted, weight],
        4_000_000_000,
        24,
    )
    few = rows // 16
    pieces = call(
        near_kernel,
        [shaped((2 * few, 1152), F32)] + [shaped((2 * few, 1152)) for _ in range(3)],
        [pltpu.VMEM((4, 2 * few, 1152), F32)],
        [ids, *got],
        1_000_000,
    )
    got = [pieces[0]] + [swap(pieces[n], "z", 2 * n) for n in range(1, 4)]
    pieces = call(
        far_kernel,
        [shaped((few, 576), F32)] + [shaped((few, 576)) for _ in range(3)],
        [],
        [ids, *got],
        1_000_000,
    )
    got = [pieces[0]] + [swap(pieces[1], "yh", 1), swap(pieces[2], "z", 1)]
    got.append(swap(pieces[3], ("yh", "z"), 9))
    (grad_weight,) = call(
        lambda *refs: last_kernel(grad_scale, *refs),
        [shaped((few, TAPS, HEAD_DIM), F32)],
        [],
        got,
        1_000_000,
    )
    return conv_out[None], grad_queries[None], grad_keys[None], grad_values[None], grad_weight


def solution(mesh):
    x, yh, z = SPLITS[mesh.shape["dp"]]
    fine = Mesh(mesh.devices.reshape(x, yh, z, 2, 2), ("x", "yh", "z", "yl", "core"))
    dp, seq = ("x", "yh", "z"), ("yl", "core")
    return jax.shard_map(
        body,
        mesh=fine,
        in_specs=(P(dp, seq, None), P(dp, seq, None), P(dp, seq, None), P(), P(dp, seq, None)),
        out_specs=(
            P(dp, seq, None),
            P(dp, seq, None),
            P(dp, seq, None),
            P(dp, seq, None),
            P(dp, None, seq),
        ),
        check_vma=False,
    )
```

```python
import math

import jax
import jax.numpy as jnp
from jax import lax
from jax.experimental import pallas as pl
from jax.experimental.pallas import tpu as pltpu
from jax.sharding import Mesh, PartitionSpec as P


HEADS = 4
HEAD_DIM = 192
TAPS = 3
STEP = 32
ROWS = 128
SPLITS = {64: (4, 2, 8), 16: (1, 2, 8)}

tanh_scale = 0.7978845608028654
cubic_term = 0.044715
norm_epsilon = 1e-06

F32 = jnp.float32
BF16 = jnp.bfloat16
WINDOW = (0, 128, 384, 512)
FIRST = (0, 64, 0, 64)
NT = (((1,), (1,)), ((), ()))
TN = (((0,), (0,)), ((), ()))


def dot(a, b, dims=(((1,), (0,)), ((), ()))):
    return lax.dot_general(a, b, dims, preferred_element_type=F32)


def masked_window(value, head):
    lane = lax.broadcasted_iota(jnp.int32, value.shape, 1)
    first = FIRST[head]
    keep = (lane >= first) & (lane < first + HEAD_DIM)
    return jnp.where(keep, value, jnp.zeros_like(value))


def window(ref, head):
    return ref[:, WINDOW[head] : WINDOW[head] + 256]


def place(parts):
    a, b, c, d = parts
    return jnp.concatenate(
        [
            a[:, :128],
            a[:, 128:] + b[:, :128],
            b[:, 128:],
            c[:, :128],
            c[:, 128:] + d[:, :128],
            d[:, 128:],
        ],
        axis=1,
    )


def gelu_value(value):
    inner = tanh_scale * (value + cubic_term * value * value * value)
    return 0.5 * value * (1.0 + jnp.tanh(inner))


def gelu_slope(value):
    square = value * value
    tangent = jnp.tanh(tanh_scale * (value + cubic_term * square * value))
    return 0.5 * (1.0 + tangent) + 0.5 * value * (1.0 - tangent * tangent) * tanh_scale * (
        1.0 + 3.0 * cubic_term * square
    )


def block_start(me, relative):
    return pl.multiple_of(jnp.bitwise_xor(me, relative) * ROWS, ROWS)


def prep_kernel(ids, *refs):
    sources, owns, (need_ref, rest_ref), sems = refs[:4], refs[4:8], refs[8:10], refs[10]
    copies = [
        pltpu.make_async_copy(source, own, sems.at[n])
        for n, (source, own) in enumerate(zip(sources, owns))
    ]
    for copy in copies:
        copy.start()
    for copy in copies:
        copy.wait()
    side = lax.div(ids[0], 2)
    need = pl.multiple_of((1 - side) * 384, 128)
    rest = pl.multiple_of(side * 384, 128)
    need_ref[...] = owns[3][:, pl.ds(need, 384)]
    rest_ref[...] = owns[3][:, pl.ds(rest, 384)]


def keys_kernel(*refs):
    k, km = refs[:4], refs[4]
    for r in range(4):
        at = slice(r * ROWS, (r + 1) * ROWS)
        for h in range(HEADS):
            km[h, at, :] = masked_window(window(k[r], h), h)


def score_kernel(*refs):
    q, km = refs[0:4], refs[4]
    soft_ref, rounded_ref = refs[5:7]
    q_all, s_ref = refs[7:]
    inverse = 1.0 / math.sqrt(HEAD_DIM)
    for r in range(4):
        q_all[r * ROWS : (r + 1) * ROWS, :] = q[r][...]
    for h in range(HEADS):
        s_ref[...] = dot(window(q_all, h), km[h], NT)
        for c in range(8):
            at = slice(c * 64, (c + 1) * 64)
            s = s_ref[at, :] * inverse
            e = jnp.exp(s - jnp.max(s, axis=1, keepdims=True))
            p = e / jnp.sum(e, axis=1, keepdims=True)
            soft_ref[h, at, :] = p
            rounded_ref[h, at, :] = p.astype(BF16)


def attend_kernel(ids, *refs):
    rounded_ref, v = refs[0], refs[1:5]
    attended_ref, acted_ref, vm = refs[5:8]
    o_ref = refs[8]
    me = ids[0]
    for r in range(4):
        at = slice(r * ROWS, (r + 1) * ROWS)
        for h in range(HEADS):
            vm[h, at, :] = masked_window(window(v[r], h), h)
    for h in range(HEADS):
        o_ref[h] = dot(rounded_ref[h], vm[h])
    acted_ref[0:STEP, :] = jnp.zeros((STEP, 768), BF16)
    acted_ref[STEP + 512 :, :] = jnp.zeros((STEP, 768), BF16)
    for r in range(4):
        at = slice(r * ROWS, (r + 1) * ROWS)
        attended = place([o_ref[h, at, :] for h in range(HEADS)]).astype(BF16)
        attended_ref[at, :] = attended
        full = attended.astype(F32)
        factor = lax.rsqrt(jnp.mean(full * full, axis=1, keepdims=True) + norm_epsilon)
        start = pl.multiple_of(block_start(me, r) + STEP, STEP)
        acted_ref[pl.ds(start, ROWS), :] = gelu_value(full * factor).astype(BF16)


def weight_kernel(ids, acted_ref, g_own, g_core, g_across, g_diag, *refs):
    outs, (slab, shifted, total) = refs[:-3], refs[-3:]
    me, mx = ids[0], ids[1]
    parts = len(outs)
    slab[0:STEP, :] = jnp.zeros((STEP, HEAD_DIM), BF16)
    slab[STEP + 512 :, :] = jnp.zeros((STEP, HEAD_DIM), BF16)
    for r, g in enumerate((g_own, g_core, g_across, g_diag)):
        mine = g[:, 0:192].astype(F32)
        count = g.shape[1] // HEAD_DIM
        for s in range(1, count):
            here = lax.rem(me, count) == s
            mine = jnp.where(here, g[:, 192 * s : 192 * s + 192].astype(F32), mine)
        start = pl.multiple_of(block_start(me, r) + STEP, STEP)
        slab[pl.ds(start, ROWS), :] = mine.astype(BF16)
    for t in range(TAPS):
        first = (2 - t) * STEP
        shifted[:, 192 * t : 192 * t + 192] = slab[first : first + 512, :]
    result = dot(acted_ref[STEP : STEP + 512, :], shifted[...], TN)
    rows = 768 // parts
    half = rows // 2
    for j in range(parts):
        total[j] = result[j * rows : (j + 1) * rows]
    for n, out in enumerate(outs):
        piece = total[jnp.bitwise_xor(mx, n)]
        out[...] = jnp.concatenate([piece[:half], piece[half:]], axis=1).astype(BF16)


def grads_kernel(ids, *refs):
    g_whole, g_need, g_rest = refs[0:2], refs[2:4], refs[4:6]
    attended_ref, acted_ref, w_ref = refs[6:9]
    conv_ref, do_ref = refs[9:11]
    g_pad, ga_ref = refs[11:]
    me = ids[0]
    own = pl.multiple_of(me * ROWS, ROWS)
    conv = jnp.zeros((ROWS, 768), F32)
    for t in range(TAPS):
        rows = acted_ref[pl.ds(pl.multiple_of(own + t * STEP, STEP), ROWS), :]
        conv = conv + dot(rows, w_ref[t])
    conv_ref[...] = conv.astype(BF16)
    g_pad[0:STEP, :] = jnp.zeros((STEP, 768), BF16)
    g_pad[STEP + 512 :, :] = jnp.zeros((STEP, 768), BF16)
    for r in range(4):
        start = pl.multiple_of(block_start(me, r) + STEP, STEP)
        if r < 2:
            g_pad[pl.ds(start, ROWS), :] = g_whole[r][...]
        else:
            side = lax.div(me, 2)
            need = pl.ds(pl.multiple_of(side * 384, 128), 384)
            rest = pl.ds(pl.multiple_of((1 - side) * 384, 128), 384)
            g_pad[pl.ds(start, ROWS), need] = g_need[r - 2][...]
            g_pad[pl.ds(start, ROWS), rest] = g_rest[r - 2][...]
    ga_ref[...] = dot(g_pad[2 * STEP : 2 * STEP + 512, :], w_ref[0], NT)
    ga_ref[...] += dot(g_pad[STEP : STEP + 512, :], w_ref[1], NT)
    ga_ref[...] += dot(g_pad[0:512, :], w_ref[2], NT)
    for r in range(4):
        at = slice(r * ROWS, (r + 1) * ROWS)
        full = attended_ref[at, :].astype(F32)
        factor = lax.rsqrt(jnp.mean(full * full, axis=1, keepdims=True) + norm_epsilon)
        normed = full * factor
        grad = ga_ref[pl.ds(block_start(me, r), ROWS), :] * gelu_slope(normed)
        inner = jnp.mean(grad * normed, axis=1, keepdims=True)
        do_ref[at, :] = (factor * (grad - normed * inner)).astype(BF16)


def backward_kernel(*refs):
    q, km, vm, soft_ref, do_ref = refs[0:4], refs[4], refs[5], refs[6], refs[7]
    dq_ref, dk_ref, dv_ref = refs[8:11]
    qm, dp_ref, ds_ref = refs[11:]
    inverse = 1.0 / math.sqrt(HEAD_DIM)
    for r in range(4):
        at = slice(r * ROWS, (r + 1) * ROWS)
        for h in range(HEADS):
            qm[h, at, :] = masked_window(window(q[r], h), h)
    dq, dk, dv = [], [], []
    for h in range(HEADS):
        grad_out = window(do_ref, h)
        dp_ref[...] = dot(grad_out, vm[h], NT)
        for c in range(8):
            at = slice(c * 64, (c + 1) * 64)
            p = soft_ref[h, at, :]
            dp = dp_ref[at, :]
            inner = jnp.sum(dp * p, axis=1, keepdims=True)
            wide = 512 if c < 2 else ROWS
            ds_ref[at, 0:wide] = (p[:, :wide] * (dp[:, :wide] - inner) * inverse).astype(BF16)
        dq.append(dot(ds_ref[0:ROWS, :], km[h]))
        dk.append(dot(ds_ref[:, 0:ROWS], qm[h], TN))
        dv.append(dot(soft_ref[h, :, 0:ROWS].astype(BF16), masked_window(grad_out, h), TN))
    dq_ref[...] = place(dq).astype(BF16)
    dk_ref[...] = place(dk).astype(BF16)
    dv_ref[...] = place(dv).astype(BF16)


def total_of(parts):
    value = parts[0][...].astype(F32)
    for part in parts[1:]:
        value = value + part[...].astype(F32)
    return value


def near_kernel(ids, *refs):
    parts, outs, total = refs[:-5], refs[-5:-1], refs[-1]
    pair = lax.div(ids[2], 2)
    value = total_of(parts)
    rows = value.shape[0] // 4
    for j in range(4):
        total[j] = value[j * rows : (j + 1) * rows]
    for n, out in enumerate(outs):
        out[...] = total[jnp.bitwise_xor(pair, n)].astype(out.dtype)


def far_kernel(ids, *refs):
    parts, outs = refs[:-4], refs[-4:]
    odd, my = lax.rem(ids[2], 2), ids[3]
    value = total_of(parts)
    few, wide = value.shape[0] // 2, value.shape[1] // 2
    rows = (value[:few], value[few:])
    for n, out in enumerate(outs):
        piece = jnp.where(odd == n // 2, rows[0], rows[1])
        piece = jnp.where(my == n % 2, piece[:, :wide], piece[:, wide:])
        out[...] = piece.astype(out.dtype)


def last_kernel(scale, *refs):
    value = total_of(refs[:-1]) * scale
    for t in range(TAPS):
        refs[-1][:, t, :] = value[:, 192 * t : 192 * t + 192]


def call(kernel, outs, scratch, args, flops, limit=16, in_hbm=()):
    size = sum(math.prod(a.shape) * a.dtype.itemsize for a in (*args, *outs))
    run = pl.pallas_call(
        kernel,
        out_shape=outs,
        in_specs=[
            pl.BlockSpec(
                memory_space=pltpu.SMEM
                if a.dtype == jnp.int32
                else pltpu.HBM
                if n in in_hbm
                else pltpu.VMEM
            )
            for n, a in enumerate(args)
        ],
        out_specs=[pl.BlockSpec(memory_space=pltpu.VMEM) for _ in outs],
        scratch_shapes=scratch,
        compiler_params=pltpu.CompilerParams(vmem_limit_bytes=limit << 20),
        cost_estimate=pl.CostEstimate(
            flops=flops, bytes_accessed=size, transcendentals=0
        ),
    )
    args = [
        pltpu.with_memory_space_constraint(a, pltpu.HBM) if n in in_hbm else a
        for n, a in enumerate(args)
    ]
    return run(*args)


def shaped(shape, dtype=BF16):
    return jax.ShapeDtypeStruct(shape, dtype)


def swap(value, axis, mask):
    count = lax.axis_size(axis)
    return lax.ppermute(value, axis, [(i, i ^ mask) for i in range(count)])


def body(queries, key_rows, value_rows, conv_weight, output_gradient):
    x_size = lax.axis_size("x")
    sizes = [lax.axis_size(a) for a in ("x", "yh", "z", "yl", "core")]
    grad_scale = 1.0 / math.sqrt(math.prod(sizes) * ROWS)
    me = lax.axis_index("yl") * 2 + lax.axis_index("core")
    ids = jnp.stack(
        [me, lax.axis_index("x"), lax.axis_index("z"), lax.axis_index("yh")]
    ).astype(jnp.int32)
    weight = jnp.transpose(conv_weight, (1, 0, 2))
    k, q, v, g = key_rows[0], queries[0], value_rows[0], output_gradient[0]
    first = {n: swap(a, "yl", 1) for n, a in (("k", k), ("q", q))}
    own_q, own_k, own_v, own_g, need, rest = call(
        prep_kernel,
        [shaped((ROWS, 768)) for _ in range(4)] + [shaped((ROWS, 384)) for _ in range(2)],
        [pltpu.SemaphoreType.DMA((4,))],
        [ids, q, k, v, g],
        1_000_000,
        in_hbm=(1, 2, 3, 4),
    )
    sent = {"v": v, "need": need, "rest": rest}
    across = first | {n: swap(a, "yl", 1) for n, a in sent.items()}
    near = {n: swap(a, "core", 1) for n, a in (("k", k), ("q", q), ("v", v), ("g", g))}
    diag = {n: swap(a, "core", 1) for n, a in across.items()}
    q = (own_q, near["q"], across["q"], diag["q"])
    k = (own_k, near["k"], across["k"], diag["k"])
    v = (own_v, near["v"], across["v"], diag["v"])
    whole = (own_g, near["g"])
    need = (across["need"], diag["need"])
    rest = (across["rest"], diag["rest"])
    (km,) = call(keys_kernel, [shaped((HEADS, 512, 256))], [], k, 1_000_000)
    soft, rounded = call(
        score_kernel,
        [shaped((HEADS, 512, 512), F32), shaped((HEADS, 512, 512))],
        [
            pltpu.VMEM((512, 768), BF16),
            pltpu.VMEM((512, 512), F32),
        ],
        [*q, km],
        1_000_000_000,
    )
    attended, acted, vm = call(
        attend_kernel,
        [shaped((512, 768)), shaped((576, 768)), shaped((HEADS, 512, 256))],
        [pltpu.VMEM((HEADS, 512, 256), F32)],
        [ids, rounded, *v],
        1_000_000_000,
    )
    rows = 768 // x_size
    pieces = call(
        weight_kernel,
        [shaped((rows // 2, 1152)) for _ in range(x_size)],
        [
            pltpu.VMEM((576, HEAD_DIM), BF16),
            pltpu.VMEM((512, 576), BF16),
            pltpu.VMEM((x_size, rows, 576), F32),
        ],
        [ids, acted, *whole, *need],
        500_000_000,
    )
    got = [pieces[0]] + [swap(pieces[n], "x", n) for n in range(1, x_size)]
    conv_out, grad_attended = call(
        grads_kernel,
        [shaped((ROWS, 768)), shaped((512, 768))],
        [pltpu.VMEM((576, 768), BF16), pltpu.VMEM((512, 768), F32)],
        [ids, *whole, *need, *rest, attended, acted, weight],
        2_000_000_000,
        20,
    )
    grad_queries, grad_keys, grad_values = call(
        backward_kernel,
        [shaped((ROWS, 768)) for _ in range(3)],
        [
            pltpu.VMEM((HEADS, 512, 256), BF16),
            pltpu.VMEM((512, 512), F32),
            pltpu.VMEM((512, 512), BF16),
        ],
        [*q, km, vm, soft, grad_attended],
        1_000_000_000,
        20,
    )
    few = rows // 16
    pieces = call(
        near_kernel,
        [shaped((2 * few, 1152), F32)] + [shaped((2 * few, 1152)) for _ in range(3)],
        [pltpu.VMEM((4, 2 * few, 1152), F32)],
        [ids, *got],
        1_000_000,
    )
    got = [pieces[0]] + [swap(pieces[n], "z", 2 * n) for n in range(1, 4)]
    pieces = call(
        far_kernel,
        [shaped((few, 576), F32)] + [shaped((few, 576)) for _ in range(3)],
        [],
        [ids, *got],
        1_000_000,
    )
    got = [pieces[0]] + [swap(pieces[1], "yh", 1), swap(pieces[2], "z", 1)]
    got.append(swap(pieces[3], ("yh", "z"), 9))
    (grad_weight,) = call(
        lambda *refs: last_kernel(grad_scale, *refs),
        [shaped((few, TAPS, HEAD_DIM), F32)],
        [],
        got,
        1_000_000,
    )
    return conv_out[None], grad_queries[None], grad_keys[None], grad_values[None], grad_weight


def solution(mesh):
    x, yh, z = SPLITS[mesh.shape["dp"]]
    fine = Mesh(mesh.devices.reshape(x, yh, z, 2, 2), ("x", "yh", "z", "yl", "core"))
    dp, seq = ("x", "yh", "z"), ("yl", "core")
    return jax.shard_map(
        body,
        mesh=fine,
        in_specs=(P(dp, seq, None), P(dp, seq, None), P(dp, seq, None), P(), P(dp, seq, None)),
        out_specs=(
            P(dp, seq, None),
            P(dp, seq, None),
            P(dp, seq, None),
            P(dp, seq, None),
            P(dp, None, seq),
        ),
        check_vma=False,
    )
```

```python
import math

import jax
import jax.numpy as jnp
from jax import lax
from jax.experimental import pallas as pl
from jax.experimental.pallas import tpu as pltpu
from jax.sharding import Mesh, PartitionSpec as P


HEADS = 4
HEAD_DIM = 192
TAPS = 3
STEP = 32
ROWS = 128
SPLITS = {64: (4, 2, 8), 16: (1, 2, 8)}

tanh_scale = 0.7978845608028654
cubic_term = 0.044715
norm_epsilon = 1e-06

F32 = jnp.float32
BF16 = jnp.bfloat16
WINDOW = (0, 128, 384, 512)
FIRST = (0, 64, 0, 64)
NT = (((1,), (1,)), ((), ()))
TN = (((0,), (0,)), ((), ()))


def dot(a, b, dims=(((1,), (0,)), ((), ()))):
    return lax.dot_general(a, b, dims, preferred_element_type=F32)


def masked_window(value, head):
    lane = lax.broadcasted_iota(jnp.int32, value.shape, 1)
    first = FIRST[head]
    keep = (lane >= first) & (lane < first + HEAD_DIM)
    return jnp.where(keep, value, jnp.zeros_like(value))


def window(ref, head):
    return ref[:, WINDOW[head] : WINDOW[head] + 256]


def place(parts):
    a, b, c, d = parts
    return jnp.concatenate(
        [
            a[:, :128],
            a[:, 128:] + b[:, :128],
            b[:, 128:],
            c[:, :128],
            c[:, 128:] + d[:, :128],
            d[:, 128:],
        ],
        axis=1,
    )


def gelu_value(value):
    inner = tanh_scale * (value + cubic_term * value * value * value)
    return 0.5 * value * (1.0 + jnp.tanh(inner))


def gelu_slope(value):
    square = value * value
    tangent = jnp.tanh(tanh_scale * (value + cubic_term * square * value))
    return 0.5 * (1.0 + tangent) + 0.5 * value * (1.0 - tangent * tangent) * tanh_scale * (
        1.0 + 3.0 * cubic_term * square
    )


def block_start(me, relative):
    return pl.multiple_of(jnp.bitwise_xor(me, relative) * ROWS, ROWS)


def prep_kernel(ids, *refs):
    sources, owns, (need_ref, rest_ref), sems = refs[:4], refs[4:8], refs[8:10], refs[10]
    copies = [
        pltpu.make_async_copy(source, own, sems.at[n])
        for n, (source, own) in enumerate(zip(sources, owns))
    ]
    for copy in copies:
        copy.start()
    for copy in copies:
        copy.wait()
    side = lax.div(ids[0], 2)
    need = pl.multiple_of((1 - side) * 384, 128)
    rest = pl.multiple_of(side * 384, 128)
    need_ref[...] = owns[3][:, pl.ds(need, 384)]
    rest_ref[...] = owns[3][:, pl.ds(rest, 384)]


def keys_kernel(*refs):
    k, km = refs[:4], refs[4]
    for r in range(4):
        at = slice(r * ROWS, (r + 1) * ROWS)
        for h in range(HEADS):
            km[h, at, :] = masked_window(window(k[r], h), h)


def score_kernel(*refs):
    q, km = refs[0:4], refs[4]
    soft_ref, rounded_ref = refs[5:7]
    q_all, s_ref = refs[7:]
    inverse = 1.0 / math.sqrt(HEAD_DIM)
    for r in range(4):
        q_all[r * ROWS : (r + 1) * ROWS, :] = q[r][...]
    for h in range(HEADS):
        s_ref[...] = dot(window(q_all, h), km[h], NT)
        for c in range(8):
            at = slice(c * 64, (c + 1) * 64)
            s = s_ref[at, :] * inverse
            e = jnp.exp(s - jnp.max(s, axis=1, keepdims=True))
            p = e / jnp.sum(e, axis=1, keepdims=True)
            soft_ref[h, at, :] = p
            rounded_ref[h, at, :] = p.astype(BF16)


def attend_kernel(ids, *refs):
    rounded_ref, v = refs[0], refs[1:5]
    attended_ref, acted_ref, vm = refs[5:8]
    o_ref = refs[8]
    me = ids[0]
    for r in range(4):
        at = slice(r * ROWS, (r + 1) * ROWS)
        for h in range(HEADS):
            vm[h, at, :] = masked_window(window(v[r], h), h)
    for h in range(HEADS):
        o_ref[h] = dot(rounded_ref[h], vm[h])
    acted_ref[0:STEP, :] = jnp.zeros((STEP, 768), BF16)
    acted_ref[STEP + 512 :, :] = jnp.zeros((STEP, 768), BF16)
    for r in range(4):
        at = slice(r * ROWS, (r + 1) * ROWS)
        attended = place([o_ref[h, at, :] for h in range(HEADS)]).astype(BF16)
        attended_ref[at, :] = attended
        full = attended.astype(F32)
        factor = lax.rsqrt(jnp.mean(full * full, axis=1, keepdims=True) + norm_epsilon)
        start = pl.multiple_of(block_start(me, r) + STEP, STEP)
        acted_ref[pl.ds(start, ROWS), :] = gelu_value(full * factor).astype(BF16)


def weight_kernel(ids, acted_ref, g_own, g_core, g_across, g_diag, *refs):
    outs, (slab, shifted, total) = refs[:-3], refs[-3:]
    me, mx = ids[0], ids[1]
    parts = len(outs)
    slab[0:STEP, :] = jnp.zeros((STEP, HEAD_DIM), BF16)
    slab[STEP + 512 :, :] = jnp.zeros((STEP, HEAD_DIM), BF16)
    for r, g in enumerate((g_own, g_core, g_across, g_diag)):
        mine = g[:, 0:192].astype(F32)
        count = g.shape[1] // HEAD_DIM
        for s in range(1, count):
            here = lax.rem(me, count) == s
            mine = jnp.where(here, g[:, 192 * s : 192 * s + 192].astype(F32), mine)
        start = pl.multiple_of(block_start(me, r) + STEP, STEP)
        slab[pl.ds(start, ROWS), :] = mine.astype(BF16)
    for t in range(TAPS):
        first = (2 - t) * STEP
        shifted[:, 192 * t : 192 * t + 192] = slab[first : first + 512, :]
    result = dot(acted_ref[STEP : STEP + 512, :], shifted[...], TN)
    rows = 768 // parts
    half = rows // 2
    for j in range(parts):
        piece = result[j * rows : (j + 1) * rows]
        total[j] = jnp.concatenate([piece[:half], piece[half:]], axis=1).astype(BF16)
    for n, out in enumerate(outs):
        out[...] = total[jnp.bitwise_xor(mx, n)]


def grads_kernel(ids, *refs):
    g_whole, g_need, g_rest = refs[0:2], refs[2:4], refs[4:6]
    attended_ref, acted_ref, w_ref = refs[6:9]
    conv_ref, do_ref = refs[9:11]
    g_pad, ga_ref = refs[11:]
    me = ids[0]
    own = pl.multiple_of(me * ROWS, ROWS)
    conv = jnp.zeros((ROWS, 768), F32)
    for t in range(TAPS):
        rows = acted_ref[pl.ds(pl.multiple_of(own + t * STEP, STEP), ROWS), :]
        conv = conv + dot(rows, w_ref[t])
    conv_ref[...] = conv.astype(BF16)
    g_pad[0:STEP, :] = jnp.zeros((STEP, 768), BF16)
    g_pad[STEP + 512 :, :] = jnp.zeros((STEP, 768), BF16)
    for r in range(4):
        start = pl.multiple_of(block_start(me, r) + STEP, STEP)
        if r < 2:
            g_pad[pl.ds(start, ROWS), :] = g_whole[r][...]
        else:
            side = lax.div(me, 2)
            need = pl.ds(pl.multiple_of(side * 384, 128), 384)
            rest = pl.ds(pl.multiple_of((1 - side) * 384, 128), 384)
            g_pad[pl.ds(start, ROWS), need] = g_need[r - 2][...]
            g_pad[pl.ds(start, ROWS), rest] = g_rest[r - 2][...]
    ga_ref[...] = dot(g_pad[2 * STEP : 2 * STEP + 512, :], w_ref[0], NT)
    ga_ref[...] += dot(g_pad[STEP : STEP + 512, :], w_ref[1], NT)
    ga_ref[...] += dot(g_pad[0:512, :], w_ref[2], NT)
    for r in range(4):
        at = slice(r * ROWS, (r + 1) * ROWS)
        full = attended_ref[at, :].astype(F32)
        factor = lax.rsqrt(jnp.mean(full * full, axis=1, keepdims=True) + norm_epsilon)
        normed = full * factor
        grad = ga_ref[pl.ds(block_start(me, r), ROWS), :] * gelu_slope(normed)
        inner = jnp.mean(grad * normed, axis=1, keepdims=True)
        do_ref[at, :] = (factor * (grad - normed * inner)).astype(BF16)


def backward_kernel(*refs):
    q, km, vm, soft_ref, do_ref = refs[0:4], refs[4], refs[5], refs[6], refs[7]
    dq_ref, dk_ref, dv_ref = refs[8:11]
    qm, dp_ref, ds_ref = refs[11:]
    inverse = 1.0 / math.sqrt(HEAD_DIM)
    for r in range(4):
        at = slice(r * ROWS, (r + 1) * ROWS)
        for h in range(HEADS):
            qm[h, at, :] = masked_window(window(q[r], h), h)
    dq, dk, dv = [], [], []
    for h in range(HEADS):
        grad_out = window(do_ref, h)
        dp_ref[...] = dot(grad_out, vm[h], NT)
        for c in range(8):
            at = slice(c * 64, (c + 1) * 64)
            p = soft_ref[h, at, :]
            dp = dp_ref[at, :]
            inner = jnp.sum(dp * p, axis=1, keepdims=True)
            wide = 512 if c < 2 else ROWS
            ds_ref[at, 0:wide] = (p[:, :wide] * (dp[:, :wide] - inner) * inverse).astype(BF16)
        dq.append(dot(ds_ref[0:ROWS, :], km[h]))
        dk.append(dot(ds_ref[:, 0:ROWS], qm[h], TN))
        dv.append(dot(soft_ref[h, :, 0:ROWS].astype(BF16), masked_window(grad_out, h), TN))
    dq_ref[...] = place(dq).astype(BF16)
    dk_ref[...] = place(dk).astype(BF16)
    dv_ref[...] = place(dv).astype(BF16)


def total_of(parts):
    value = parts[0][...].astype(F32)
    for part in parts[1:]:
        value = value + part[...].astype(F32)
    return value


def near_kernel(ids, *refs):
    parts, outs, total = refs[:-5], refs[-5:-1], refs[-1]
    pair = lax.div(ids[2], 2)
    value = total_of(parts)
    rows = value.shape[0] // 4
    for j in range(4):
        total[j] = value[j * rows : (j + 1) * rows]
    for n, out in enumerate(outs):
        out[...] = total[jnp.bitwise_xor(pair, n)].astype(out.dtype)


def far_kernel(ids, *refs):
    parts, outs = refs[:-4], refs[-4:]
    odd, my = lax.rem(ids[2], 2), ids[3]
    value = total_of(parts)
    few, wide = value.shape[0] // 2, value.shape[1] // 2
    rows = (value[:few], value[few:])
    for n, out in enumerate(outs):
        piece = jnp.where(odd == n // 2, rows[0], rows[1])
        piece = jnp.where(my == n % 2, piece[:, :wide], piece[:, wide:])
        out[...] = piece.astype(out.dtype)


def last_kernel(scale, *refs):
    value = total_of(refs[:-1]) * scale
    for t in range(TAPS):
        refs[-1][:, t, :] = value[:, 192 * t : 192 * t + 192]


def call(kernel, outs, scratch, args, flops, limit=16, in_hbm=()):
    size = sum(math.prod(a.shape) * a.dtype.itemsize for a in (*args, *outs))
    run = pl.pallas_call(
        kernel,
        out_shape=outs,
        in_specs=[
            pl.BlockSpec(
                memory_space=pltpu.SMEM
                if a.dtype == jnp.int32
                else pltpu.HBM
                if n in in_hbm
                else pltpu.VMEM
            )
            for n, a in enumerate(args)
        ],
        out_specs=[pl.BlockSpec(memory_space=pltpu.VMEM) for _ in outs],
        scratch_shapes=scratch,
        compiler_params=pltpu.CompilerParams(vmem_limit_bytes=limit << 20),
        cost_estimate=pl.CostEstimate(
            flops=flops, bytes_accessed=size, transcendentals=0
        ),
    )
    args = [
        pltpu.with_memory_space_constraint(a, pltpu.HBM) if n in in_hbm else a
        for n, a in enumerate(args)
    ]
    return run(*args)


def shaped(shape, dtype=BF16):
    return jax.ShapeDtypeStruct(shape, dtype)


def swap(value, axis, mask):
    count = lax.axis_size(axis)
    return lax.ppermute(value, axis, [(i, i ^ mask) for i in range(count)])


def body(queries, key_rows, value_rows, conv_weight, output_gradient):
    x_size = lax.axis_size("x")
    sizes = [lax.axis_size(a) for a in ("x", "yh", "z", "yl", "core")]
    grad_scale = 1.0 / math.sqrt(math.prod(sizes) * ROWS)
    me = lax.axis_index("yl") * 2 + lax.axis_index("core")
    ids = jnp.stack(
        [me, lax.axis_index("x"), lax.axis_index("z"), lax.axis_index("yh")]
    ).astype(jnp.int32)
    weight = jnp.transpose(conv_weight, (1, 0, 2))
    k, q, v, g = key_rows[0], queries[0], value_rows[0], output_gradient[0]
    first = {n: swap(a, "yl", 1) for n, a in (("k", k), ("q", q))}
    own_q, own_k, own_v, own_g, need, rest = call(
        prep_kernel,
        [shaped((ROWS, 768)) for _ in range(4)] + [shaped((ROWS, 384)) for _ in range(2)],
        [pltpu.SemaphoreType.DMA((4,))],
        [ids, q, k, v, g],
        1_000_000,
        in_hbm=(1, 2, 3, 4),
    )
    sent = {"v": v, "need": need, "rest": rest}
    across = first | {n: swap(a, "yl", 1) for n, a in sent.items()}
    near = {n: swap(a, "core", 1) for n, a in (("k", k), ("q", q), ("v", v), ("g", g))}
    diag = {n: swap(a, "core", 1) for n, a in across.items()}
    q = (own_q, near["q"], across["q"], diag["q"])
    k = (own_k, near["k"], across["k"], diag["k"])
    v = (own_v, near["v"], across["v"], diag["v"])
    whole = (own_g, near["g"])
    need = (across["need"], diag["need"])
    rest = (across["rest"], diag["rest"])
    (km,) = call(keys_kernel, [shaped((HEADS, 512, 256))], [], k, 1_000_000)
    soft, rounded = call(
        score_kernel,
        [shaped((HEADS, 512, 512), F32), shaped((HEADS, 512, 512))],
        [
            pltpu.VMEM((512, 768), BF16),
            pltpu.VMEM((512, 512), F32),
        ],
        [*q, km],
        1_000_000_000,
    )
    attended, acted, vm = call(
        attend_kernel,
        [shaped((512, 768)), shaped((576, 768)), shaped((HEADS, 512, 256))],
        [pltpu.VMEM((HEADS, 512, 256), F32)],
        [ids, rounded, *v],
        1_000_000_000,
    )
    rows = 768 // x_size
    pieces = call(
        weight_kernel,
        [shaped((rows // 2, 1152)) for _ in range(x_size)],
        [
            pltpu.VMEM((576, HEAD_DIM), BF16),
            pltpu.VMEM((512, 576), BF16),
            pltpu.VMEM((x_size, rows // 2, 1152), BF16),
        ],
        [ids, acted, *whole, *need],
        500_000_000,
    )
    got = [pieces[0]] + [swap(pieces[n], "x", n) for n in range(1, x_size)]
    conv_out, grad_attended = call(
        grads_kernel,
        [shaped((ROWS, 768)), shaped((512, 768))],
        [pltpu.VMEM((576, 768), BF16), pltpu.VMEM((512, 768), F32)],
        [ids, *whole, *need, *rest, attended, acted, weight],
        2_000_000_000,
        20,
    )
    grad_queries, grad_keys, grad_values = call(
        backward_kernel,
        [shaped((ROWS, 768)) for _ in range(3)],
        [
            pltpu.VMEM((HEADS, 512, 256), BF16),
            pltpu.VMEM((512, 512), F32),
            pltpu.VMEM((512, 512), BF16),
        ],
        [*q, km, vm, soft, grad_attended],
        1_000_000_000,
        20,
    )
    few = rows // 16
    pieces = call(
        near_kernel,
        [shaped((2 * few, 1152), F32)] + [shaped((2 * few, 1152)) for _ in range(3)],
        [pltpu.VMEM((4, 2 * few, 1152), F32)],
        [ids, *got],
        1_000_000,
    )
    got = [pieces[0]] + [swap(pieces[n], "z", 2 * n) for n in range(1, 4)]
    pieces = call(
        far_kernel,
        [shaped((few, 576), F32)] + [shaped((few, 576)) for _ in range(3)],
        [],
        [ids, *got],
        1_000_000,
    )
    got = [pieces[0]] + [swap(pieces[1], "yh", 1), swap(pieces[2], "z", 1)]
    got.append(swap(pieces[3], ("yh", "z"), 9))
    (grad_weight,) = call(
        lambda *refs: last_kernel(grad_scale, *refs),
        [shaped((few, TAPS, HEAD_DIM), F32)],
        [],
        got,
        1_000_000,
    )
    return conv_out[None], grad_queries[None], grad_keys[None], grad_values[None], grad_weight


def solution(mesh):
    x, yh, z = SPLITS[mesh.shape["dp"]]
    fine = Mesh(mesh.devices.reshape(x, yh, z, 2, 2), ("x", "yh", "z", "yl", "core"))
    dp, seq = ("x", "yh", "z"), ("yl", "core")
    return jax.shard_map(
        body,
        mesh=fine,
        in_specs=(P(dp, seq, None), P(dp, seq, None), P(dp, seq, None), P(), P(dp, seq, None)),
        out_specs=(
            P(dp, seq, None),
            P(dp, seq, None),
            P(dp, seq, None),
            P(dp, seq, None),
            P(dp, None, seq),
        ),
        check_vma=False,
    )
```

```python
import math

import jax
import jax.numpy as jnp
from jax import lax
from jax.experimental import pallas as pl
from jax.experimental.pallas import tpu as pltpu
from jax.sharding import Mesh, PartitionSpec as P


HEADS = 4
HEAD_DIM = 192
TAPS = 3
STEP = 32
ROWS = 128
SPLITS = {64: (4, 2, 8), 16: (1, 2, 8)}

tanh_scale = 0.7978845608028654
cubic_term = 0.044715
norm_epsilon = 1e-06

F32 = jnp.float32
BF16 = jnp.bfloat16
WINDOW = (0, 128, 384, 512)
FIRST = (0, 64, 0, 64)
NT = (((1,), (1,)), ((), ()))
TN = (((0,), (0,)), ((), ()))


def dot(a, b, dims=(((1,), (0,)), ((), ()))):
    return lax.dot_general(a, b, dims, preferred_element_type=F32)


def masked_window(value, head):
    lane = lax.broadcasted_iota(jnp.int32, value.shape, 1)
    first = FIRST[head]
    keep = (lane >= first) & (lane < first + HEAD_DIM)
    return jnp.where(keep, value, jnp.zeros_like(value))


def window(ref, head):
    return ref[:, WINDOW[head] : WINDOW[head] + 256]


def place(parts):
    a, b, c, d = parts
    return jnp.concatenate(
        [
            a[:, :128],
            a[:, 128:] + b[:, :128],
            b[:, 128:],
            c[:, :128],
            c[:, 128:] + d[:, :128],
            d[:, 128:],
        ],
        axis=1,
    )


def gelu_value(value):
    inner = tanh_scale * (value + cubic_term * value * value * value)
    return 0.5 * value * (1.0 + jnp.tanh(inner))


def gelu_slope(value):
    square = value * value
    tangent = jnp.tanh(tanh_scale * (value + cubic_term * square * value))
    return 0.5 * (1.0 + tangent) + 0.5 * value * (1.0 - tangent * tangent) * tanh_scale * (
        1.0 + 3.0 * cubic_term * square
    )


def block_start(me, relative):
    return pl.multiple_of(jnp.bitwise_xor(me, relative) * ROWS, ROWS)


def prep_kernel(ids, *refs):
    sources, owns, (need_ref, rest_ref), sems = refs[:4], refs[4:8], refs[8:10], refs[10]
    copies = [
        pltpu.make_async_copy(source, own, sems.at[n])
        for n, (source, own) in enumerate(zip(sources, owns))
    ]
    for copy in copies:
        copy.start()
    for copy in copies:
        copy.wait()
    side = lax.div(ids[0], 2)
    need = pl.multiple_of((1 - side) * 384, 128)
    rest = pl.multiple_of(side * 384, 128)
    need_ref[...] = owns[3][:, pl.ds(need, 384)]
    rest_ref[...] = owns[3][:, pl.ds(rest, 384)]


def keys_kernel(*refs):
    k, km = refs[:4], refs[4]
    for r in range(4):
        at = slice(r * ROWS, (r + 1) * ROWS)
        for h in range(HEADS):
            km[h, at, :] = masked_window(window(k[r], h), h)


def score_kernel(*refs):
    q, km = refs[:-5], refs[-5]
    soft_ref, rounded_ref, q_all, s_ref = refs[-4:]
    inverse = 1.0 / math.sqrt(HEAD_DIM)
    for r, block in enumerate(q):
        q_all[r * ROWS : (r + 1) * ROWS, :] = block[...]
    for h in range(HEADS):
        s_ref[...] = dot(window(q_all, h), km[h], NT)
        for c in range(2 * len(q)):
            at = slice(c * 64, (c + 1) * 64)
            s = s_ref[at, :] * inverse
            e = jnp.exp(s - jnp.max(s, axis=1, keepdims=True))
            p = e / jnp.sum(e, axis=1, keepdims=True)
            soft_ref[h, at, :] = p
            rounded_ref[h, at, :] = p.astype(BF16)


def attend_kernel(ids, *refs):
    rounded, v = refs[0:2], refs[2:6]
    attended_ref, acted_ref, vm = refs[6:9]
    o_ref = refs[9]
    me = ids[0]
    for r in range(4):
        at = slice(r * ROWS, (r + 1) * ROWS)
        for h in range(HEADS):
            vm[h, at, :] = masked_window(window(v[r], h), h)
    for h in range(HEADS):
        weights = jnp.concatenate([part[h] for part in rounded], axis=0)
        o_ref[h] = dot(weights, vm[h])
    acted_ref[0:STEP, :] = jnp.zeros((STEP, 768), BF16)
    acted_ref[STEP + 512 :, :] = jnp.zeros((STEP, 768), BF16)
    for r in range(4):
        at = slice(r * ROWS, (r + 1) * ROWS)
        attended = place([o_ref[h, at, :] for h in range(HEADS)]).astype(BF16)
        attended_ref[at, :] = attended
        full = attended.astype(F32)
        factor = lax.rsqrt(jnp.mean(full * full, axis=1, keepdims=True) + norm_epsilon)
        start = pl.multiple_of(block_start(me, r) + STEP, STEP)
        acted_ref[pl.ds(start, ROWS), :] = gelu_value(full * factor).astype(BF16)


def weight_kernel(ids, acted_ref, g_own, g_core, g_across, g_diag, *refs):
    outs, (slab, shifted, total) = refs[:-3], refs[-3:]
    me, mx = ids[0], ids[1]
    parts = len(outs)
    slab[0:STEP, :] = jnp.zeros((STEP, HEAD_DIM), BF16)
    slab[STEP + 512 :, :] = jnp.zeros((STEP, HEAD_DIM), BF16)
    for r, g in enumerate((g_own, g_core, g_across, g_diag)):
        mine = g[:, 0:192].astype(F32)
        count = g.shape[1] // HEAD_DIM
        for s in range(1, count):
            here = lax.rem(me, count) == s
            mine = jnp.where(here, g[:, 192 * s : 192 * s + 192].astype(F32), mine)
        start = pl.multiple_of(block_start(me, r) + STEP, STEP)
        slab[pl.ds(start, ROWS), :] = mine.astype(BF16)
    for t in range(TAPS):
        first = (2 - t) * STEP
        shifted[:, 192 * t : 192 * t + 192] = slab[first : first + 512, :]
    result = dot(acted_ref[STEP : STEP + 512, :], shifted[...], TN)
    rows = 768 // parts
    half = rows // 2
    for j in range(parts):
        piece = result[j * rows : (j + 1) * rows]
        total[j] = jnp.concatenate([piece[:half], piece[half:]], axis=1).astype(BF16)
    for n, out in enumerate(outs):
        out[...] = total[jnp.bitwise_xor(mx, n)]


def grads_kernel(ids, *refs):
    g_whole, g_need, g_rest = refs[0:2], refs[2:4], refs[4:6]
    attended_ref, acted_ref, w_ref = refs[6:9]
    conv_ref, do_ref = refs[9:11]
    g_pad, ga_ref = refs[11:]
    me = ids[0]
    own = pl.multiple_of(me * ROWS, ROWS)
    conv = jnp.zeros((ROWS, 768), F32)
    for t in range(TAPS):
        rows = acted_ref[pl.ds(pl.multiple_of(own + t * STEP, STEP), ROWS), :]
        conv = conv + dot(rows, w_ref[t])
    conv_ref[...] = conv.astype(BF16)
    g_pad[0:STEP, :] = jnp.zeros((STEP, 768), BF16)
    g_pad[STEP + 512 :, :] = jnp.zeros((STEP, 768), BF16)
    for r in range(4):
        start = pl.multiple_of(block_start(me, r) + STEP, STEP)
        if r < 2:
            g_pad[pl.ds(start, ROWS), :] = g_whole[r][...]
        else:
            side = lax.div(me, 2)
            need = pl.ds(pl.multiple_of(side * 384, 128), 384)
            rest = pl.ds(pl.multiple_of((1 - side) * 384, 128), 384)
            g_pad[pl.ds(start, ROWS), need] = g_need[r - 2][...]
            g_pad[pl.ds(start, ROWS), rest] = g_rest[r - 2][...]
    ga_ref[...] = dot(g_pad[2 * STEP : 2 * STEP + 512, :], w_ref[0], NT)
    ga_ref[...] += dot(g_pad[STEP : STEP + 512, :], w_ref[1], NT)
    ga_ref[...] += dot(g_pad[0:512, :], w_ref[2], NT)
    for r in range(4):
        at = slice(r * ROWS, (r + 1) * ROWS)
        full = attended_ref[at, :].astype(F32)
        factor = lax.rsqrt(jnp.mean(full * full, axis=1, keepdims=True) + norm_epsilon)
        normed = full * factor
        grad = ga_ref[pl.ds(block_start(me, r), ROWS), :] * gelu_slope(normed)
        inner = jnp.mean(grad * normed, axis=1, keepdims=True)
        do_ref[at, :] = (factor * (grad - normed * inner)).astype(BF16)


def backward_kernel(*refs):
    q, km, vm, soft, do_ref = refs[0:4], refs[4], refs[5], refs[6:8], refs[8]
    dq_ref, dk_ref, dv_ref = refs[9:12]
    qm, dp_ref, ds_ref = refs[12:]
    inverse = 1.0 / math.sqrt(HEAD_DIM)
    for r in range(4):
        at = slice(r * ROWS, (r + 1) * ROWS)
        for h in range(HEADS):
            qm[h, at, :] = masked_window(window(q[r], h), h)
    dq, dk, dv = [], [], []
    for h in range(HEADS):
        grad_out = window(do_ref, h)
        dp_ref[...] = dot(grad_out, vm[h], NT)
        for c in range(8):
            at = slice(c * 64, (c + 1) * 64)
            p = soft[c // 6][h, (c % 6) * 64 : (c % 6) * 64 + 64, :]
            dp = dp_ref[at, :]
            inner = jnp.sum(dp * p, axis=1, keepdims=True)
            wide = 512 if c < 2 else ROWS
            ds_ref[at, 0:wide] = (p[:, :wide] * (dp[:, :wide] - inner) * inverse).astype(BF16)
        dq.append(dot(ds_ref[0:ROWS, :], km[h]))
        dk.append(dot(ds_ref[:, 0:ROWS], qm[h], TN))
        weights = jnp.concatenate([part[h, :, 0:ROWS].astype(BF16) for part in soft], axis=0)
        dv.append(dot(weights, masked_window(grad_out, h), TN))
    dq_ref[...] = place(dq).astype(BF16)
    dk_ref[...] = place(dk).astype(BF16)
    dv_ref[...] = place(dv).astype(BF16)


def total_of(parts):
    value = parts[0][...].astype(F32)
    for part in parts[1:]:
        value = value + part[...].astype(F32)
    return value


def near_kernel(ids, *refs):
    parts, outs, total = refs[:-5], refs[-5:-1], refs[-1]
    pair = lax.div(ids[2], 2)
    value = total_of(parts)
    rows = value.shape[0] // 4
    for j in range(4):
        total[j] = value[j * rows : (j + 1) * rows]
    for n, out in enumerate(outs):
        out[...] = total[jnp.bitwise_xor(pair, n)].astype(out.dtype)


def far_kernel(ids, *refs):
    parts, outs = refs[:-4], refs[-4:]
    odd, my = lax.rem(ids[2], 2), ids[3]
    value = total_of(parts)
    few, wide = value.shape[0] // 2, value.shape[1] // 2
    rows = (value[:few], value[few:])
    for n, out in enumerate(outs):
        piece = jnp.where(odd == n // 2, rows[0], rows[1])
        piece = jnp.where(my == n % 2, piece[:, :wide], piece[:, wide:])
        out[...] = piece.astype(out.dtype)


def last_kernel(scale, *refs):
    value = total_of(refs[:-1]) * scale
    for t in range(TAPS):
        refs[-1][:, t, :] = value[:, 192 * t : 192 * t + 192]


def call(kernel, outs, scratch, args, flops, limit=16, in_hbm=()):
    size = sum(math.prod(a.shape) * a.dtype.itemsize for a in (*args, *outs))
    run = pl.pallas_call(
        kernel,
        out_shape=outs,
        in_specs=[
            pl.BlockSpec(
                memory_space=pltpu.SMEM
                if a.dtype == jnp.int32
                else pltpu.HBM
                if n in in_hbm
                else pltpu.VMEM
            )
            for n, a in enumerate(args)
        ],
        out_specs=[pl.BlockSpec(memory_space=pltpu.VMEM) for _ in outs],
        scratch_shapes=scratch,
        compiler_params=pltpu.CompilerParams(vmem_limit_bytes=limit << 20),
        cost_estimate=pl.CostEstimate(
            flops=flops, bytes_accessed=size, transcendentals=0
        ),
    )
    args = [
        pltpu.with_memory_space_constraint(a, pltpu.HBM) if n in in_hbm else a
        for n, a in enumerate(args)
    ]
    return run(*args)


def shaped(shape, dtype=BF16):
    return jax.ShapeDtypeStruct(shape, dtype)


def swap(value, axis, mask):
    count = lax.axis_size(axis)
    return lax.ppermute(value, axis, [(i, i ^ mask) for i in range(count)])


def body(queries, key_rows, value_rows, conv_weight, output_gradient):
    x_size = lax.axis_size("x")
    sizes = [lax.axis_size(a) for a in ("x", "yh", "z", "yl", "core")]
    grad_scale = 1.0 / math.sqrt(math.prod(sizes) * ROWS)
    me = lax.axis_index("yl") * 2 + lax.axis_index("core")
    ids = jnp.stack(
        [me, lax.axis_index("x"), lax.axis_index("z"), lax.axis_index("yh")]
    ).astype(jnp.int32)
    weight = jnp.transpose(conv_weight, (1, 0, 2))
    k, q, v, g = key_rows[0], queries[0], value_rows[0], output_gradient[0]
    first = {n: swap(a, "yl", 1) for n, a in (("k", k), ("q", q))}
    own_q, own_k, own_v, own_g, need, rest = call(
        prep_kernel,
        [shaped((ROWS, 768)) for _ in range(4)] + [shaped((ROWS, 384)) for _ in range(2)],
        [pltpu.SemaphoreType.DMA((4,))],
        [ids, q, k, v, g],
        1_000_000,
        in_hbm=(1, 2, 3, 4),
    )
    sent = {"v": v, "need": need, "rest": rest}
    across = first | {n: swap(a, "yl", 1) for n, a in sent.items()}
    near = {n: swap(a, "core", 1) for n, a in (("k", k), ("q", q), ("v", v), ("g", g))}
    diag = {n: swap(a, "core", 1) for n, a in across.items()}
    q = (own_q, near["q"], across["q"], diag["q"])
    k = (own_k, near["k"], across["k"], diag["k"])
    v = (own_v, near["v"], across["v"], diag["v"])
    whole = (own_g, near["g"])
    need = (across["need"], diag["need"])
    rest = (across["rest"], diag["rest"])
    (km,) = call(keys_kernel, [shaped((HEADS, 512, 256))], [], k, 1_000_000)
    soft, rounded = [], []
    for part in (q[:3], q[3:]):
        rows = ROWS * len(part)
        exact, low = call(
            score_kernel,
            [shaped((HEADS, rows, 512), F32), shaped((HEADS, rows, 512))],
            [pltpu.VMEM((rows, 768), BF16), pltpu.VMEM((rows, 512), F32)],
            [*part, km],
            2_000_000 * rows,
        )
        soft.append(exact)
        rounded.append(low)
    attended, acted, vm = call(
        attend_kernel,
        [shaped((512, 768)), shaped((576, 768)), shaped((HEADS, 512, 256))],
        [pltpu.VMEM((HEADS, 512, 256), F32)],
        [ids, *rounded, *v],
        1_000_000_000,
    )
    rows = 768 // x_size
    pieces = call(
        weight_kernel,
        [shaped((rows // 2, 1152)) for _ in range(x_size)],
        [
            pltpu.VMEM((576, HEAD_DIM), BF16),
            pltpu.VMEM((512, 576), BF16),
            pltpu.VMEM((x_size, rows // 2, 1152), BF16),
        ],
        [ids, acted, *whole, *need],
        500_000_000,
    )
    got = [pieces[0]] + [swap(pieces[n], "x", n) for n in range(1, x_size)]
    conv_out, grad_attended = call(
        grads_kernel,
        [shaped((ROWS, 768)), shaped((512, 768))],
        [pltpu.VMEM((576, 768), BF16), pltpu.VMEM((512, 768), F32)],
        [ids, *whole, *need, *rest, attended, acted, weight],
        2_000_000_000,
        20,
    )
    grad_queries, grad_keys, grad_values = call(
        backward_kernel,
        [shaped((ROWS, 768)) for _ in range(3)],
        [
            pltpu.VMEM((HEADS, 512, 256), BF16),
            pltpu.VMEM((512, 512), F32),
            pltpu.VMEM((512, 512), BF16),
        ],
        [*q, km, vm, *soft, grad_attended],
        1_000_000_000,
        20,
    )
    few = rows // 16
    pieces = call(
        near_kernel,
        [shaped((2 * few, 1152), F32)] + [shaped((2 * few, 1152)) for _ in range(3)],
        [pltpu.VMEM((4, 2 * few, 1152), F32)],
        [ids, *got],
        1_000_000,
    )
    got = [pieces[0]] + [swap(pieces[n], "z", 2 * n) for n in range(1, 4)]
    pieces = call(
        far_kernel,
        [shaped((few, 576), F32)] + [shaped((few, 576)) for _ in range(3)],
        [],
        [ids, *got],
        1_000_000,
    )
    got = [pieces[0]] + [swap(pieces[1], "yh", 1), swap(pieces[2], "z", 1)]
    got.append(swap(pieces[3], ("yh", "z"), 9))
    (grad_weight,) = call(
        lambda *refs: last_kernel(grad_scale, *refs),
        [shaped((few, TAPS, HEAD_DIM), F32)],
        [],
        got,
        1_000_000,
    )
    return conv_out[None], grad_queries[None], grad_keys[None], grad_values[None], grad_weight


def solution(mesh):
    x, yh, z = SPLITS[mesh.shape["dp"]]
    fine = Mesh(mesh.devices.reshape(x, yh, z, 2, 2), ("x", "yh", "z", "yl", "core"))
    dp, seq = ("x", "yh", "z"), ("yl", "core")
    return jax.shard_map(
        body,
        mesh=fine,
        in_specs=(P(dp, seq, None), P(dp, seq, None), P(dp, seq, None), P(), P(dp, seq, None)),
        out_specs=(
            P(dp, seq, None),
            P(dp, seq, None),
            P(dp, seq, None),
            P(dp, seq, None),
            P(dp, None, seq),
        ),
        check_vma=False,
    )
```

```python
import math

import jax
import jax.numpy as jnp
from jax import lax
from jax.experimental import pallas as pl
from jax.experimental.pallas import tpu as pltpu
from jax.sharding import Mesh, PartitionSpec as P


HEADS = 4
HEAD_DIM = 192
TAPS = 3
STEP = 32
ROWS = 128
SPLITS = {64: (4, 2, 8), 16: (1, 2, 8)}

tanh_scale = 0.7978845608028654
cubic_term = 0.044715
norm_epsilon = 1e-06

F32 = jnp.float32
BF16 = jnp.bfloat16
WINDOW = (0, 128, 384, 512)
FIRST = (0, 64, 0, 64)
NT = (((1,), (1,)), ((), ()))
TN = (((0,), (0,)), ((), ()))


def dot(a, b, dims=(((1,), (0,)), ((), ()))):
    return lax.dot_general(a, b, dims, preferred_element_type=F32)


def masked_window(value, head):
    lane = lax.broadcasted_iota(jnp.int32, value.shape, 1)
    first = FIRST[head]
    keep = (lane >= first) & (lane < first + HEAD_DIM)
    return jnp.where(keep, value, jnp.zeros_like(value))


def window(ref, head):
    return ref[:, WINDOW[head] : WINDOW[head] + 256]


def place(parts):
    a, b, c, d = parts
    return jnp.concatenate(
        [
            a[:, :128],
            a[:, 128:] + b[:, :128],
            b[:, 128:],
            c[:, :128],
            c[:, 128:] + d[:, :128],
            d[:, 128:],
        ],
        axis=1,
    )


def gelu_value(value):
    inner = tanh_scale * (value + cubic_term * value * value * value)
    return 0.5 * value * (1.0 + jnp.tanh(inner))


def gelu_slope(value):
    square = value * value
    tangent = jnp.tanh(tanh_scale * (value + cubic_term * square * value))
    return 0.5 * (1.0 + tangent) + 0.5 * value * (1.0 - tangent * tangent) * tanh_scale * (
        1.0 + 3.0 * cubic_term * square
    )


def block_start(me, relative):
    return pl.multiple_of(jnp.bitwise_xor(me, relative) * ROWS, ROWS)


def prep_kernel(ids, *refs):
    sources, owns, (need_ref, rest_ref), sems = refs[:4], refs[4:8], refs[8:10], refs[10]
    copies = [
        pltpu.make_async_copy(source, own, sems.at[n])
        for n, (source, own) in enumerate(zip(sources, owns))
    ]
    for copy in copies:
        copy.start()
    for copy in copies:
        copy.wait()
    side = lax.div(ids[0], 2)
    need = pl.multiple_of((1 - side) * 384, 128)
    rest = pl.multiple_of(side * 384, 128)
    need_ref[...] = owns[3][:, pl.ds(need, 384)]
    rest_ref[...] = owns[3][:, pl.ds(rest, 384)]


def keys_kernel(*refs):
    k, km = refs[:4], refs[4]
    for r in range(4):
        at = slice(r * ROWS, (r + 1) * ROWS)
        for h in range(HEADS):
            km[h, at, :] = masked_window(window(k[r], h), h)


def score_kernel(*refs):
    q, km = refs[0:4], refs[4]
    soft_ref, rounded_ref = refs[5:7]
    q_all, s_ref = refs[7:]
    inverse = 1.0 / math.sqrt(HEAD_DIM)
    for r in range(4):
        q_all[r * ROWS : (r + 1) * ROWS, :] = q[r][...]
    for h in range(HEADS):
        s_ref[...] = dot(window(q_all, h), km[h], NT)
        for c in range(8):
            at = slice(c * 64, (c + 1) * 64)
            s = s_ref[at, :] * inverse
            e = jnp.exp(s - jnp.max(s, axis=1, keepdims=True))
            p = e / jnp.sum(e, axis=1, keepdims=True)
            soft_ref[h, at, :] = p
            rounded_ref[h, at, :] = p.astype(BF16)


def begin_kernel(rounded_ref, v_own, v_core, vm, o_ref):
    for r, block in enumerate((v_own, v_core)):
        for h in range(HEADS):
            vm[h, r * ROWS : (r + 1) * ROWS, :] = masked_window(window(block, h), h)
    for h in range(HEADS):
        o_ref[h] = dot(rounded_ref[h, :, 0:256], vm[h])


def attend_kernel(ids, rounded_ref, begun_ref, v_across, v_diag, *refs):
    attended_ref, acted_ref, vm, o_ref = refs
    me = ids[0]
    for r, block in enumerate((v_across, v_diag)):
        for h in range(HEADS):
            vm[h, r * ROWS : (r + 1) * ROWS, :] = masked_window(window(block, h), h)
    for h in range(HEADS):
        o_ref[h] = begun_ref[h] + dot(rounded_ref[h, :, 256:512], vm[h])
    acted_ref[0:STEP, :] = jnp.zeros((STEP, 768), BF16)
    acted_ref[STEP + 512 :, :] = jnp.zeros((STEP, 768), BF16)
    for r in range(4):
        at = slice(r * ROWS, (r + 1) * ROWS)
        attended = place([o_ref[h, at, :] for h in range(HEADS)]).astype(BF16)
        attended_ref[at, :] = attended
        full = attended.astype(F32)
        factor = lax.rsqrt(jnp.mean(full * full, axis=1, keepdims=True) + norm_epsilon)
        start = pl.multiple_of(block_start(me, r) + STEP, STEP)
        acted_ref[pl.ds(start, ROWS), :] = gelu_value(full * factor).astype(BF16)


def weight_kernel(ids, acted_ref, g_own, g_core, g_across, g_diag, *refs):
    outs, (slab, shifted, total) = refs[:-3], refs[-3:]
    me, mx = ids[0], ids[1]
    parts = len(outs)
    slab[0:STEP, :] = jnp.zeros((STEP, HEAD_DIM), BF16)
    slab[STEP + 512 :, :] = jnp.zeros((STEP, HEAD_DIM), BF16)
    for r, g in enumerate((g_own, g_core, g_across, g_diag)):
        mine = g[:, 0:192].astype(F32)
        count = g.shape[1] // HEAD_DIM
        for s in range(1, count):
            here = lax.rem(me, count) == s
            mine = jnp.where(here, g[:, 192 * s : 192 * s + 192].astype(F32), mine)
        start = pl.multiple_of(block_start(me, r) + STEP, STEP)
        slab[pl.ds(start, ROWS), :] = mine.astype(BF16)
    for t in range(TAPS):
        first = (2 - t) * STEP
        shifted[:, 192 * t : 192 * t + 192] = slab[first : first + 512, :]
    result = dot(acted_ref[STEP : STEP + 512, :], shifted[...], TN)
    rows = 768 // parts
    half = rows // 2
    for j in range(parts):
        piece = result[j * rows : (j + 1) * rows]
        total[j] = jnp.concatenate([piece[:half], piece[half:]], axis=1).astype(BF16)
    for n, out in enumerate(outs):
        out[...] = total[jnp.bitwise_xor(mx, n)]


def conv_kernel(ids, acted_ref, w_ref, conv_ref):
    own = pl.multiple_of(ids[0] * ROWS, ROWS)
    conv = jnp.zeros((ROWS, 768), F32)
    for t in range(TAPS):
        rows = acted_ref[pl.ds(pl.multiple_of(own + t * STEP, STEP), ROWS), :]
        conv = conv + dot(rows, w_ref[t])
    conv_ref[...] = conv.astype(BF16)


def grads_kernel(ids, *refs):
    g_whole, g_need, g_rest = refs[0:2], refs[2:4], refs[4:6]
    attended_ref, w_ref, do_ref, g_pad, ga_ref = refs[6:]
    me = ids[0]
    g_pad[0:STEP, :] = jnp.zeros((STEP, 768), BF16)
    g_pad[STEP + 512 :, :] = jnp.zeros((STEP, 768), BF16)
    for r in range(4):
        start = pl.multiple_of(block_start(me, r) + STEP, STEP)
        if r < 2:
            g_pad[pl.ds(start, ROWS), :] = g_whole[r][...]
        else:
            side = lax.div(me, 2)
            need = pl.ds(pl.multiple_of(side * 384, 128), 384)
            rest = pl.ds(pl.multiple_of((1 - side) * 384, 128), 384)
            g_pad[pl.ds(start, ROWS), need] = g_need[r - 2][...]
            g_pad[pl.ds(start, ROWS), rest] = g_rest[r - 2][...]
    ga_ref[...] = dot(g_pad[2 * STEP : 2 * STEP + 512, :], w_ref[0], NT)
    ga_ref[...] += dot(g_pad[STEP : STEP + 512, :], w_ref[1], NT)
    ga_ref[...] += dot(g_pad[0:512, :], w_ref[2], NT)
    for r in range(4):
        at = slice(r * ROWS, (r + 1) * ROWS)
        full = attended_ref[at, :].astype(F32)
        factor = lax.rsqrt(jnp.mean(full * full, axis=1, keepdims=True) + norm_epsilon)
        normed = full * factor
        grad = ga_ref[pl.ds(block_start(me, r), ROWS), :] * gelu_slope(normed)
        inner = jnp.mean(grad * normed, axis=1, keepdims=True)
        do_ref[at, :] = (factor * (grad - normed * inner)).astype(BF16)


def backward_kernel(*refs):
    q, km, vm, soft_ref, do_ref = refs[0:4], refs[4], refs[5:7], refs[7], refs[8]
    dq_ref, dk_ref, dv_ref = refs[9:12]
    qm, dp_ref, ds_ref = refs[12:]
    inverse = 1.0 / math.sqrt(HEAD_DIM)
    for r in range(4):
        at = slice(r * ROWS, (r + 1) * ROWS)
        for h in range(HEADS):
            qm[h, at, :] = masked_window(window(q[r], h), h)
    dq, dk, dv = [], [], []
    for h in range(HEADS):
        grad_out = window(do_ref, h)
        dp_ref[:, 0:256] = dot(grad_out, vm[0][h], NT)
        dp_ref[:, 256:512] = dot(grad_out, vm[1][h], NT)
        for c in range(8):
            at = slice(c * 64, (c + 1) * 64)
            p = soft_ref[h, at, :]
            dp = dp_ref[at, :]
            inner = jnp.sum(dp * p, axis=1, keepdims=True)
            wide = 512 if c < 2 else ROWS
            ds_ref[at, 0:wide] = (p[:, :wide] * (dp[:, :wide] - inner) * inverse).astype(BF16)
        dq.append(dot(ds_ref[0:ROWS, :], km[h]))
        dk.append(dot(ds_ref[:, 0:ROWS], qm[h], TN))
        dv.append(dot(soft_ref[h, :, 0:ROWS].astype(BF16), masked_window(grad_out, h), TN))
    dq_ref[...] = place(dq).astype(BF16)
    dk_ref[...] = place(dk).astype(BF16)
    dv_ref[...] = place(dv).astype(BF16)


def total_of(parts):
    value = parts[0][...].astype(F32)
    for part in parts[1:]:
        value = value + part[...].astype(F32)
    return value


def near_kernel(ids, *refs):
    parts, outs, total = refs[:-5], refs[-5:-1], refs[-1]
    pair = lax.div(ids[2], 2)
    value = total_of(parts)
    rows = value.shape[0] // 4
    for j in range(4):
        total[j] = value[j * rows : (j + 1) * rows]
    for n, out in enumerate(outs):
        out[...] = total[jnp.bitwise_xor(pair, n)].astype(out.dtype)


def far_kernel(ids, *refs):
    parts, outs = refs[:-4], refs[-4:]
    odd, my = lax.rem(ids[2], 2), ids[3]
    value = total_of(parts)
    few, wide = value.shape[0] // 2, value.shape[1] // 2
    rows = (value[:few], value[few:])
    for n, out in enumerate(outs):
        piece = jnp.where(odd == n // 2, rows[0], rows[1])
        piece = jnp.where(my == n % 2, piece[:, :wide], piece[:, wide:])
        out[...] = piece.astype(out.dtype)


def last_kernel(scale, *refs):
    value = total_of(refs[:-1]) * scale
    for t in range(TAPS):
        refs[-1][:, t, :] = value[:, 192 * t : 192 * t + 192]


def call(kernel, outs, scratch, args, flops, limit=16, in_hbm=()):
    size = sum(math.prod(a.shape) * a.dtype.itemsize for a in (*args, *outs))
    run = pl.pallas_call(
        kernel,
        out_shape=outs,
        in_specs=[
            pl.BlockSpec(
                memory_space=pltpu.SMEM
                if a.dtype == jnp.int32
                else pltpu.HBM
                if n in in_hbm
                else pltpu.VMEM
            )
            for n, a in enumerate(args)
        ],
        out_specs=[pl.BlockSpec(memory_space=pltpu.VMEM) for _ in outs],
        scratch_shapes=scratch,
        compiler_params=pltpu.CompilerParams(vmem_limit_bytes=limit << 20),
        cost_estimate=pl.CostEstimate(
            flops=flops, bytes_accessed=size, transcendentals=0
        ),
    )
    args = [
        pltpu.with_memory_space_constraint(a, pltpu.HBM) if n in in_hbm else a
        for n, a in enumerate(args)
    ]
    return run(*args)


def shaped(shape, dtype=BF16):
    return jax.ShapeDtypeStruct(shape, dtype)


def swap(value, axis, mask):
    count = lax.axis_size(axis)
    return lax.ppermute(value, axis, [(i, i ^ mask) for i in range(count)])


def body(queries, key_rows, value_rows, conv_weight, output_gradient):
    x_size = lax.axis_size("x")
    sizes = [lax.axis_size(a) for a in ("x", "yh", "z", "yl", "core")]
    grad_scale = 1.0 / math.sqrt(math.prod(sizes) * ROWS)
    me = lax.axis_index("yl") * 2 + lax.axis_index("core")
    ids = jnp.stack(
        [me, lax.axis_index("x"), lax.axis_index("z"), lax.axis_index("yh")]
    ).astype(jnp.int32)
    weight = jnp.transpose(conv_weight, (1, 0, 2))
    k, q, v, g = key_rows[0], queries[0], value_rows[0], output_gradient[0]
    first = {n: swap(a, "yl", 1) for n, a in (("k", k), ("q", q))}
    own_q, own_k, own_v, own_g, need, rest = call(
        prep_kernel,
        [shaped((ROWS, 768)) for _ in range(4)] + [shaped((ROWS, 384)) for _ in range(2)],
        [pltpu.SemaphoreType.DMA((4,))],
        [ids, q, k, v, g],
        1_000_000,
        in_hbm=(1, 2, 3, 4),
    )
    sent = {"v": v, "need": need, "rest": rest}
    across = first | {n: swap(a, "yl", 1) for n, a in sent.items()}
    near = {n: swap(a, "core", 1) for n, a in (("k", k), ("q", q), ("v", v), ("g", g))}
    diag = {n: swap(a, "core", 1) for n, a in across.items()}
    q = (own_q, near["q"], across["q"], diag["q"])
    k = (own_k, near["k"], across["k"], diag["k"])
    v = (own_v, near["v"], across["v"], diag["v"])
    whole = (own_g, near["g"])
    need = (across["need"], diag["need"])
    rest = (across["rest"], diag["rest"])
    (km,) = call(keys_kernel, [shaped((HEADS, 512, 256))], [], k, 1_000_000)
    soft, rounded = call(
        score_kernel,
        [shaped((HEADS, 512, 512), F32), shaped((HEADS, 512, 512))],
        [
            pltpu.VMEM((512, 768), BF16),
            pltpu.VMEM((512, 512), F32),
        ],
        [*q, km],
        1_000_000_000,
    )
    vm_near, begun = call(
        begin_kernel,
        [shaped((HEADS, 256, 256)), shaped((HEADS, 512, 256), F32)],
        [],
        [rounded, *v[:2]],
        500_000_000,
    )
    attended, acted, vm_far = call(
        attend_kernel,
        [shaped((512, 768)), shaped((576, 768)), shaped((HEADS, 256, 256))],
        [pltpu.VMEM((HEADS, 512, 256), F32)],
        [ids, rounded, begun, *v[2:]],
        500_000_000,
    )
    rows = 768 // x_size
    pieces = call(
        weight_kernel,
        [shaped((rows // 2, 1152)) for _ in range(x_size)],
        [
            pltpu.VMEM((576, HEAD_DIM), BF16),
            pltpu.VMEM((512, 576), BF16),
            pltpu.VMEM((x_size, rows // 2, 1152), BF16),
        ],
        [ids, acted, *whole, *need],
        500_000_000,
    )
    got = [pieces[0]] + [swap(pieces[n], "x", n) for n in range(1, x_size)]
    (conv_out,) = call(conv_kernel, [shaped((ROWS, 768))], [], [ids, acted, weight], 500_000_000)
    (grad_attended,) = call(
        grads_kernel,
        [shaped((512, 768))],
        [pltpu.VMEM((576, 768), BF16), pltpu.VMEM((512, 768), F32)],
        [ids, *whole, *need, *rest, attended, weight],
        2_000_000_000,
        20,
    )
    grad_queries, grad_keys, grad_values = call(
        backward_kernel,
        [shaped((ROWS, 768)) for _ in range(3)],
        [
            pltpu.VMEM((HEADS, 512, 256), BF16),
            pltpu.VMEM((512, 512), F32),
            pltpu.VMEM((512, 512), BF16),
        ],
        [*q, km, vm_near, vm_far, soft, grad_attended],
        1_000_000_000,
        20,
    )
    few = rows // 16
    pieces = call(
        near_kernel,
        [shaped((2 * few, 1152), F32)] + [shaped((2 * few, 1152)) for _ in range(3)],
        [pltpu.VMEM((4, 2 * few, 1152), F32)],
        [ids, *got],
        1_000_000,
    )
    got = [pieces[0]] + [swap(pieces[n], "z", 2 * n) for n in range(1, 4)]
    pieces = call(
        far_kernel,
        [shaped((few, 576), F32)] + [shaped((few, 576)) for _ in range(3)],
        [],
        [ids, *got],
        1_000_000,
    )
    got = [pieces[0]] + [swap(pieces[1], "yh", 1), swap(pieces[2], "z", 1)]
    got.append(swap(pieces[3], ("yh", "z"), 9))
    (grad_weight,) = call(
        lambda *refs: last_kernel(grad_scale, *refs),
        [shaped((few, TAPS, HEAD_DIM), F32)],
        [],
        got,
        1_000_000,
    )
    return conv_out[None], grad_queries[None], grad_keys[None], grad_values[None], grad_weight


def solution(mesh):
    x, yh, z = SPLITS[mesh.shape["dp"]]
    fine = Mesh(mesh.devices.reshape(x, yh, z, 2, 2), ("x", "yh", "z", "yl", "core"))
    dp, seq = ("x", "yh", "z"), ("yl", "core")
    return jax.shard_map(
        body,
        mesh=fine,
        in_specs=(P(dp, seq, None), P(dp, seq, None), P(dp, seq, None), P(), P(dp, seq, None)),
        out_specs=(
            P(dp, seq, None),
            P(dp, seq, None),
            P(dp, seq, None),
            P(dp, seq, None),
            P(dp, None, seq),
        ),
        check_vma=False,
    )
```
